32 devices in a mesh: stream: 8 (over z, x), cross: 4 (over y, core).
Axes of the slice: x: 2, y: 2, z: 4, core: 2. Of those that a mesh axis runs over, the one named last changes fastest.
Arguments:
- adjoint: float32 [5, 32, 4096], P(None, 'stream', 'cross'), may hold values from -6 to 6
- source: float32 [5, 32, 4096], P(None, 'stream', 'cross'), may hold values from -30 to 30
- shape_grad: float32 [5, 32, 4096], P(None, 'stream', 'cross'), may hold values from -6 to 6
- lower_band: float32 [2, 5, 32, 4096], P(None, None, 'stream', 'cross'), may hold values from -1.5 to 0.5
- upper_band: float32 [3, 5, 32, 4096], P(None, None, 'stream', 'cross'), may hold values from -6 to 2, as said below
- jacobian: float32 [5, 5], replicated, may hold values from -2.5 to 2.5
- left_vectors: float32 [5, 5], replicated, may hold values from -1 to 2
- right_vectors: float32 [5, 5], replicated, may hold values from -1 to 2
- ctrl_local: int32 [32, 4096], P('stream', 'cross'), may hold values from 0 to 65535
Outputs:
- adjoint_next: float32 [5, 32, 4096], P(None, 'stream', 'cross')
- sensitivity: float32 [524288], P(('stream', 'cross'))
The draws below stay inside these ranges and needn't reach their ends.
Inputs may be any that keep to these rules, and one draw needn't show every extreme that they name: upper_band[0] lies in 0.5 to 2.
All inputs are finite; a program needn't handle non-finite values.
Results may differ from the reference program's by a relative error of at most 0.00029.
Values sent between devices are 32-bit elements; how exact they have to be, the bound alone decides.
No kernel may reach another device: no remote copies, remote signals or barrier semaphores. Data moves between devices by JAX's collectives and lax.ppermute only.
A program may use at most 64 MiB of HBM per device.

```python
import jax
import jax.numpy as jnp
from jax import lax

NF = 5
NI_DEV = 4
NCTRL = 524288
NI = 32
NJ = 4096
NCTRL_SLAB = 65536


def draw_source(key, part):
    position = (jnp.arange(NI, dtype=jnp.float32) + 0.5) / NI
    growth = jnp.exp(jnp.log(3.0) * position)[None, :, None]
    rough = jnp.clip(jax.random.normal(jax.random.fold_in(key, 1), (NF, NI, NJ), jnp.float32), -8.0, 8.0)
    return rough * growth


def slow_rates(key, low, high):
    return jax.random.uniform(key, (NF, NI, NJ), jnp.float32, low, high)


def draw_lower_band(key, part):
    slow = slow_rates(jax.random.fold_in(key, 11), 0.8, 0.99)
    fast = jax.random.uniform(jax.random.fold_in(key, 12), (NF, 1, NJ), jnp.float32, 0.1, 0.5)
    fast = jnp.broadcast_to(fast, (NF, NI, NJ))
    return jnp.stack([-(slow + fast), slow * fast])


def draw_upper_band(key, part):
    slow = slow_rates(jax.random.fold_in(key, 21), 0.8, 0.99)
    fast = jax.random.uniform(jax.random.fold_in(key, 22), (NF, 1, NJ), jnp.float32, 0.1, 0.5)
    fast = jnp.broadcast_to(fast, (NF, NI, NJ))
    diagonal = jnp.exp(jax.random.uniform(jax.random.fold_in(key, 23), (NF, NI, NJ), jnp.float32, jnp.log(0.5), jnp.log(2.0)))
    return jnp.stack([diagonal, -(slow + fast) * diagonal, slow * fast * diagonal])


def draw_left_vectors(key, part):
    noise = jnp.clip(jax.random.normal(jax.random.fold_in(key, 31), (NF, NF), jnp.float32), -3.0, 3.0)
    return jnp.eye(NF, dtype=jnp.float32) + 0.3 * noise


def draw_right_vectors(key, part):
    noise = jnp.clip(jax.random.normal(jax.random.fold_in(key, 41), (NF, NF), jnp.float32), -3.0, 3.0)
    return jnp.eye(NF, dtype=jnp.float32) + 0.3 * noise


def plant(drawn, own_key, least, high):
    index_at = [jax.random.randint(jax.random.fold_in(own_key, axis), (), 0, length) for axis, length in enumerate(drawn.shape)]
    widest = drawn.shape.index(max(drawn.shape))
    neighbour = index_at[:widest] + [(index_at[widest] + 1) % drawn.shape[widest]] + index_at[widest + 1:]
    return drawn.at[tuple(index_at)].set(least).at[tuple(neighbour)].set(high)


def steps_of(stream_key, extent, shards, least, high):
    level = 1.0
    for axis_at, shards_of in shards:
        steps = jax.random.uniform(jax.random.fold_in(jax.random.fold_in(stream_key, 6), axis_at), (shards_of,), jnp.float32, least / len(shards), high / len(shards))
        level = level * jnp.repeat(jnp.exp(steps), extent[axis_at] // shards_of).reshape((-1,) + (1,) * (len(extent) - 1 - axis_at))
    return level


def scatter_about(key, shape, scale, most, pieces=(), kind=jnp.bfloat16):
    array = jax.random.normal(key, shape, jnp.float32) * scale
    if len(pieces) > 0:
        array = steps_of(key, shape, pieces, -0.22, 0.18) * array
    return jnp.clip(array, min=-most, max=most).astype(kind)


def setup_inputs(seed: int = 0) -> dict:
    key_of = jax.random.split(jax.random.key(seed), 10)
    adjoint = scatter_about(key_of[0], (NF, NI, NJ), 1.0, 6.0, ((1, 8), (2, 4)), jnp.float32)
    source = draw_source(jax.random.fold_in(key_of[9], 71), 0)
    shape_grad = scatter_about(key_of[2], (NF, NI, NJ), 1.0, 6.0, ((1, 8), (2, 4)), jnp.float32)
    lower_band = draw_lower_band(jax.random.fold_in(key_of[9], 71), 0)
    upper_band = draw_upper_band(jax.random.fold_in(key_of[9], 71), 0)
    jacobian = scatter_about(key_of[5], (NF, NF), NF ** -0.5, 2.5, (), jnp.float32)
    left_vectors = draw_left_vectors(jax.random.fold_in(key_of[9], 71), 0)
    right_vectors = draw_right_vectors(jax.random.fold_in(key_of[9], 71), 0)
    ctrl_local = plant(jax.random.randint(key_of[8], (NI, NJ), 0, NCTRL_SLAB), jax.random.fold_in(key_of[8], 1), 0, NCTRL_SLAB - 1).astype(jnp.int32)
    return {"adjoint": adjoint, "source": source, "shape_grad": shape_grad, "lower_band": lower_band, "upper_band": upper_band, "jacobian": jacobian, "left_vectors": left_vectors, "right_vectors": right_vectors, "ctrl_local": ctrl_local}


dissipation = 0.25
step_scale = 0.5
epsilon = 1e-06

def reference(adjoint, source, shape_grad, lower_band, upper_band, jacobian, left_vectors, right_vectors, ctrl_local):
    highest = lax.Precision.HIGHEST
    padded = jnp.pad(adjoint, ((0, 0), (1, 1), (0, 0)))
    ahead_cells = padded[:, 2:, :]
    behind = padded[:, :-2, :]
    central = jnp.einsum('fg,gij->fij', jacobian, ahead_cells - behind, precision=highest)
    residual = source - 0.5 * central + dissipation * (ahead_cells - 2.0 * adjoint + behind)
    characteristic = jnp.einsum('fg,gij->fij', left_vectors, residual, precision=highest)

    def forward_step(previous, inputs):
        rhs_cell, first_sub, second_sub = inputs
        value = rhs_cell - first_sub * previous[0] - second_sub * previous[1]
        return ((value, previous[0]), value)
    start = jnp.zeros((NF, NJ), jnp.float32)
    moved = (jnp.moveaxis(characteristic, 1, 0), jnp.moveaxis(lower_band[0], 1, 0), jnp.moveaxis(lower_band[1], 1, 0))
    _, forward = lax.scan(forward_step, (start, start), moved)

    def backward_step(previous, inputs):
        rhs_cell, diag_cell, first_sup, second_sup = inputs
        value = (rhs_cell - first_sup * previous[0] - second_sup * previous[1]) / diag_cell
        return ((value, previous[0]), value)
    moved_back = (forward, jnp.moveaxis(upper_band[0], 1, 0), jnp.moveaxis(upper_band[1], 1, 0), jnp.moveaxis(upper_band[2], 1, 0))
    _, solved = lax.scan(backward_step, (start, start), moved_back, reverse=True)
    solved = jnp.moveaxis(solved, 0, 1)
    increment = jnp.einsum('fg,gij->fij', right_vectors, solved, precision=highest)
    squares = jnp.sum(increment * increment)
    root_mean = jnp.sqrt(squares / (NF * NI * NJ) + epsilon)
    adjoint_next = adjoint + step_scale * increment / root_mean
    contribution = lax.optimization_barrier(jnp.sum(adjoint * shape_grad, axis=0))
    slab_index = (jnp.arange(NI, dtype=jnp.int32) // NI_DEV).astype(jnp.int32)
    control_point = (slab_index[:, None] * NCTRL_SLAB + ctrl_local).astype(jnp.int32)
    sensitivity = jax.ops.segment_sum(contribution.ravel(), control_point.ravel(), num_segments=NCTRL)
    return (adjoint_next, sensitivity)
```

```python
import functools

import jax
import jax.numpy as jnp
from jax import lax
from jax.experimental import pallas as pl
from jax.experimental.pallas import tpu as pltpu
from jax.sharding import PartitionSpec as P

NCTRL = 524288
LANES = 128
SUBLANES = 8

dissipation = 0.25
step_scale = 0.5
epsilon = 1e-06

VMEM = pl.BlockSpec(memory_space=pltpu.VMEM)
SMEM = pl.BlockSpec(memory_space=pltpu.SMEM)


def round_up(value, step):
    return -(-value // step) * step


def mix(matrix_ref, columns):
    count = len(columns)
    return [
        sum(matrix_ref[f, g] * columns[g] for g in range(1, count)) + matrix_ref[f, 0] * columns[0]
        for f in range(count)
    ]


CELL_KINDS = 5


def block_rows(fields, cells):
    return round_up(fields * (CELL_KINDS * cells + cells - 1 + 2), SUBLANES)


def pack_kernel(parts, width, jac, left, adj, src, low, up, out, pad):
    fields, cells, length = adj.shape
    rows = block_rows(fields, cells)
    if width < LANES or rows > fields * (CELL_KINDS * cells + cells + 1):
        out[...] = jnp.zeros_like(out)
    pad[...] = jnp.zeros_like(pad)
    for f in range(fields):
        pad[f, 1 : cells + 1, :] = adj[f]
    ahead = [pad[f, 2 : cells + 2, :] for f in range(fields)]
    behind = [pad[f, 0:cells, :] for f in range(fields)]
    central = mix(jac, [a - b for a, b in zip(ahead, behind)])
    residual = [
        src[f] - 0.5 * central[f] + dissipation * (ahead[f] - 2.0 * adj[f] + behind[f])
        for f in range(fields)
    ]
    characteristic = mix(left, residual)
    cell = lax.broadcasted_iota(jnp.int32, (cells, length), 0)
    extra = CELL_KINDS * fields * cells
    for f in range(fields):
        diagonal = up[0, f]
        inverse = 1.0 / diagonal
        own = jnp.where(cell == 1, inverse, 1.0)
        diagonal_1 = jnp.broadcast_to(up[0, f, 1:2, :], (cells, length))
        values = (
            characteristic[f] * own,
            low[0, f] * jnp.where(cell == 2, diagonal_1, own),
            low[1, f] * jnp.where(cell == 3, diagonal_1, own),
            up[1, f] * inverse,
            up[2, f] * inverse,
        )
        for d in range(parts):
            lanes = slice(d * width, (d + 1) * width)
            for k, value in enumerate(values):
                at = (k * fields + f) * cells
                out[d, at : at + cells, 0:width] = value[:, lanes]
            at = extra + f * (cells + 1)
            out[d, at : at + 1, 0:width] = inverse[0:1, lanes]
            out[d, at + 1 : at + cells - 1, 0:width] = inverse[2:cells, lanes]
            out[d, at + cells - 1 : at + cells, 0:width] = adj[f, 0:1, lanes]
            out[d, at + cells : at + cells + 1, 0:width] = adj[f, cells - 1 : cells, lanes]


def solve_kernel(parts, fields, cells, jac, left, right, lines, out, edge, whole):
    rows = block_rows(fields, cells)
    back = round_up(fields * cells + 1, SUBLANES)
    extra = CELL_KINDS * fields * cells

    def across(row):
        return lines[pl.ds(row, parts, stride=rows), :]

    firsts = [across(extra + f * (cells + 1) + cells - 1) for f in range(fields)]
    lasts = [across(extra + f * (cells + 1) + cells) for f in range(fields)]
    from_last = mix(jac, lasts)
    from_first = mix(jac, firsts)
    into_first = mix(left, [0.5 * a + dissipation * b for a, b in zip(from_last, lasts)])
    into_last = mix(left, [dissipation * b - 0.5 * a for a, b in zip(from_first, firsts)])
    for f in range(fields):
        edge[f * parts : (f + 1) * parts, :] = into_first[f]
        edge[(fields + f) * parts : (fields + f + 1) * parts, :] = into_last[f]

    def kind(d, k, i):
        return lines[pl.ds(d * rows + k * fields * cells + i, fields, stride=cells), :]

    def inverse(d, i):
        at = d * rows + extra + (i if i == 0 else i - 1)
        return lines[pl.ds(at, fields, stride=cells + 1), :]

    forward = {}
    one = two = None
    for d in range(parts):
        for i in range(cells):
            value = kind(d, 0, i)
            if i == 0 and d > 0:
                value = value + edge[pl.ds(d - 1, fields, stride=parts), :]
            if i == cells - 1 and d < parts - 1:
                value = value + edge[pl.ds(fields * parts + d + 1, fields, stride=parts), :]
            if two is not None:
                value = value - kind(d, 2, i) * two
            if one is not None:
                value = value - kind(d, 1, i) * one
            forward[d, i] = value
            one, two = value, one
    one = two = None
    total = parts * cells
    for d in reversed(range(parts)):
        for i in reversed(range(cells)):
            value = forward[d, i] if i == 1 else forward[d, i] * inverse(d, i)
            if two is not None:
                value = value - kind(d, 4, i) * two
            if one is not None:
                value = value - kind(d, 3, i) * one
            whole[pl.ds(d * cells + i, fields, stride=total), :] = value
            one, two = value, one
    increment = mix(right, [whole[g * total : (g + 1) * total, :] for g in range(fields)])
    squares = sum(v * v for v in increment[1:]) + increment[0] * increment[0]
    squares = jnp.broadcast_to(jnp.sum(squares, axis=0, keepdims=True), (back - fields * cells, LANES))
    for d in range(parts):
        for f in range(fields):
            at = d * back + f * cells
            out[at : at + cells, :] = increment[f][d * cells : (d + 1) * cells, :]
        out[d * back + fields * cells : (d + 1) * back, :] = squares


def slab_kernel(peers, me, adj, grad, ctrl, *outs):
    fields, cells, length = adj.shape
    height = outs[0].shape[0]
    contribution = adj[0] * grad[0]
    for f in range(1, fields):
        contribution = contribution + adj[f] * grad[f]
    upper = contribution.astype(jnp.bfloat16).astype(jnp.float32)
    lower = contribution - upper
    high = lax.shift_right_logical(ctrl[...], 7)
    low = lax.bitwise_and(ctrl[...], LANES - 1)
    block = lax.broadcasted_iota(jnp.int32, (height, length), 0)
    lane = lax.broadcasted_iota(jnp.int32, (LANES, length), 0)
    sums = None
    for i in range(cells):
        hit = lane == low[i : i + 1, :]
        terms = jnp.concatenate(
            [
                jnp.where(hit, upper[i : i + 1, :], 0.0).astype(jnp.bfloat16),
                jnp.where(hit, lower[i : i + 1, :], 0.0).astype(jnp.bfloat16),
            ],
            axis=0,
        )
        rows = []
        for k in range(peers):
            offset = lax.bitwise_xor(me[0], k) * height
            rows.append(jnp.where(block == high[i : i + 1, :] - offset, 1.0, 0.0).astype(jnp.bfloat16))
        picked = jnp.concatenate(rows, axis=0)
        part = lax.dot_general(
            picked, terms, (((1,), (1,)), ((), ())), preferred_element_type=jnp.float32
        )
        sums = part if sums is None else sums + part
    sums = sums[:, :LANES] + sums[:, LANES:]
    for k in range(peers):
        outs[k][...] = sums[k * height : (k + 1) * height, :]


def finish_kernel(parts, width, peers, cell_count, adj, moved, *refs):
    squares, blocks, (out, sens) = refs[:peers], refs[peers : 2 * peers], refs[2 * peers :]
    fields, cells, _ = adj.shape
    back = moved.shape[0] // parts
    total = squares[0][...]
    slab = blocks[0][...]
    for k in range(1, peers):
        total = total + squares[k][...]
        slab = slab + blocks[k][...]
    sens[...] = slab
    total = jnp.sum(jnp.sum(total, axis=0, keepdims=True), axis=1, keepdims=True)
    factor = step_scale / jnp.sqrt(total / cell_count + epsilon)
    for d in range(parts):
        lanes = slice(d * width, (d + 1) * width)
        for f in range(fields):
            at = d * back + f * cells
            out[f, :, lanes] = adj[f, :, lanes] + factor * moved[at : at + cells, 0:width]


def shards(
    adjoint, source, shape_grad, lower_band, upper_band, jacobian, left_vectors, right_vectors, ctrl_local
):
    fields, cells, length = adjoint.shape
    parts, peers = lax.axis_size("stream"), lax.axis_size("cross")
    width = length // parts
    rows = block_rows(fields, cells)
    back = round_up(fields * cells + 1, SUBLANES)
    f32 = jnp.float32

    packed = pl.pallas_call(
        functools.partial(pack_kernel, parts, width),
        out_shape=jax.ShapeDtypeStruct((parts, rows, LANES), f32),
        in_specs=[SMEM, SMEM, VMEM, VMEM, VMEM, VMEM],
        out_specs=VMEM,
        scratch_shapes=[pltpu.VMEM((fields, round_up(cells + 2, SUBLANES), length), f32)],
        name="pack",
    )(jacobian, left_vectors, adjoint, source, lower_band, upper_band)
    lines = lax.all_to_all(
        packed.reshape(parts * rows, LANES), "stream", split_axis=0, concat_axis=0, tiled=True
    )

    height = NCTRL // (parts * peers * LANES)
    me = lax.axis_index("cross").astype(jnp.int32).reshape(1)
    blocks = pl.pallas_call(
        functools.partial(slab_kernel, peers),
        out_shape=[jax.ShapeDtypeStruct((height, LANES), f32)] * peers,
        in_specs=[SMEM, VMEM, VMEM, VMEM],
        out_specs=[VMEM] * peers,
        cost_estimate=pl.CostEstimate(
            flops=4 * cells * length * NCTRL // parts, bytes_accessed=4 << 20, transcendentals=0
        ),
        name="slab",
    )(me, adjoint, shape_grad, ctrl_local)

    def exchange(arrays):
        return [arrays[0]] + [
            lax.ppermute(arrays[k], "cross", [(i, i ^ k) for i in range(peers)])
            for k in range(1, peers)
        ]

    blocks = exchange(blocks)

    moved = pl.pallas_call(
        functools.partial(solve_kernel, parts, fields, cells),
        out_shape=jax.ShapeDtypeStruct((parts * back, LANES), f32),
        in_specs=[SMEM, SMEM, SMEM, VMEM],
        out_specs=VMEM,
        scratch_shapes=[
            pltpu.VMEM((2 * fields * parts, LANES), f32),
            pltpu.VMEM((fields * parts * cells, LANES), f32),
        ],
        name="solve",
    )(jacobian, left_vectors, right_vectors, lines)
    moved = lax.all_to_all(moved, "stream", split_axis=0, concat_axis=0, tiled=True)
    squares = moved.reshape(parts, back, LANES)[:, fields * cells, :]
    squares = exchange([squares] * peers)

    cell_count = fields * cells * length * parts * peers
    adjoint_next, sensitivity = pl.pallas_call(
        functools.partial(finish_kernel, parts, width, peers, cell_count),
        out_shape=[
            jax.ShapeDtypeStruct(adjoint.shape, f32),
            jax.ShapeDtypeStruct((height, LANES), f32),
        ],
        in_specs=[VMEM] * (2 + 2 * peers),
        out_specs=[VMEM, VMEM],
        name="finish",
    )(adjoint, moved, *squares, *blocks)
    return adjoint_next, sensitivity.reshape(height * LANES)


def solution(mesh):
    in_specs = (
        P(None, "stream", "cross"),
        P(None, "stream", "cross"),
        P(None, "stream", "cross"),
        P(None, None, "stream", "cross"),
        P(None, None, "stream", "cross"),
        P(),
        P(),
        P(),
        P("stream", "cross"),
    )
    out_specs = (P(None, "stream", "cross"), P(("stream", "cross")))
    return jax.shard_map(shards, mesh=mesh, in_specs=in_specs, out_specs=out_specs, check_vma=False)
```

```python
import functools

import jax
import jax.numpy as jnp
from jax import lax
from jax.experimental import pallas as pl
from jax.experimental.pallas import tpu as pltpu
from jax.sharding import PartitionSpec as P

NCTRL = 524288
LANES = 128
SUBLANES = 8

dissipation = 0.25
step_scale = 0.5
epsilon = 1e-06

VMEM = pl.BlockSpec(memory_space=pltpu.VMEM)
SMEM = pl.BlockSpec(memory_space=pltpu.SMEM)


def held(array):
    return pltpu.with_memory_space_constraint(array, pltpu.VMEM)


def round_up(value, step):
    return -(-value // step) * step


def mix(matrix_ref, columns):
    count = len(columns)
    return [
        sum(matrix_ref[f, g] * columns[g] for g in range(1, count)) + matrix_ref[f, 0] * columns[0]
        for f in range(count)
    ]


CELL_KINDS = 5


def block_rows(fields, cells):
    return round_up(fields * (CELL_KINDS * cells + cells - 1 + 2), SUBLANES)


def pack_kernel(parts, width, jac, left, adj, src, low, up, out, pad):
    fields, cells, length = adj.shape
    rows = block_rows(fields, cells)
    if width < LANES or rows > fields * (CELL_KINDS * cells + cells + 1):
        out[...] = jnp.zeros_like(out)
    pad[...] = jnp.zeros_like(pad)
    for f in range(fields):
        pad[f, 1 : cells + 1, :] = adj[f]
    ahead = [pad[f, 2 : cells + 2, :] for f in range(fields)]
    behind = [pad[f, 0:cells, :] for f in range(fields)]
    central = mix(jac, [a - b for a, b in zip(ahead, behind)])
    residual = [
        src[f] - 0.5 * central[f] + dissipation * (ahead[f] - 2.0 * adj[f] + behind[f])
        for f in range(fields)
    ]
    characteristic = mix(left, residual)
    cell = lax.broadcasted_iota(jnp.int32, (cells, length), 0)
    extra = CELL_KINDS * fields * cells
    for f in range(fields):
        diagonal = up[0, f]
        inverse = 1.0 / diagonal
        own = jnp.where(cell == 1, inverse, 1.0)
        diagonal_1 = jnp.broadcast_to(up[0, f, 1:2, :], (cells, length))
        values = (
            characteristic[f] * own,
            low[0, f] * jnp.where(cell == 2, diagonal_1, own),
            low[1, f] * jnp.where(cell == 3, diagonal_1, own),
            up[1, f] * inverse,
            up[2, f] * inverse,
        )
        for d in range(parts):
            lanes = slice(d * width, (d + 1) * width)
            for k, value in enumerate(values):
                at = (k * fields + f) * cells
                out[d, at : at + cells, 0:width] = value[:, lanes]
            at = extra + f * (cells + 1)
            out[d, at : at + 1, 0:width] = inverse[0:1, lanes]
            out[d, at + 1 : at + cells - 1, 0:width] = inverse[2:cells, lanes]
            out[d, at + cells - 1 : at + cells, 0:width] = adj[f, 0:1, lanes]
            out[d, at + cells : at + cells + 1, 0:width] = adj[f, cells - 1 : cells, lanes]


def solve_kernel(parts, fields, cells, jac, left, right, lines, out, edge, whole):
    rows = block_rows(fields, cells)
    back = round_up(fields * cells + 1, SUBLANES)
    extra = CELL_KINDS * fields * cells

    def across(row):
        return lines[pl.ds(row, parts, stride=rows), :]

    firsts = [across(extra + f * (cells + 1) + cells - 1) for f in range(fields)]
    lasts = [across(extra + f * (cells + 1) + cells) for f in range(fields)]
    from_last = mix(jac, lasts)
    from_first = mix(jac, firsts)
    into_first = mix(left, [0.5 * a + dissipation * b for a, b in zip(from_last, lasts)])
    into_last = mix(left, [dissipation * b - 0.5 * a for a, b in zip(from_first, firsts)])
    for f in range(fields):
        edge[f * parts : (f + 1) * parts, :] = into_first[f]
        edge[(fields + f) * parts : (fields + f + 1) * parts, :] = into_last[f]

    def kind(d, k, i):
        return lines[pl.ds(d * rows + k * fields * cells + i, fields, stride=cells), :]

    def inverse(d, i):
        at = d * rows + extra + (i if i == 0 else i - 1)
        return lines[pl.ds(at, fields, stride=cells + 1), :]

    forward = {}
    one = two = None
    for d in range(parts):
        for i in range(cells):
            value = kind(d, 0, i)
            if i == 0 and d > 0:
                value = value + edge[pl.ds(d - 1, fields, stride=parts), :]
            if i == cells - 1 and d < parts - 1:
                value = value + edge[pl.ds(fields * parts + d + 1, fields, stride=parts), :]
            if two is not None:
                value = value - kind(d, 2, i) * two
            if one is not None:
                value = value - kind(d, 1, i) * one
            forward[d, i] = value
            one, two = value, one
    one = two = None
    total = parts * cells
    for d in reversed(range(parts)):
        for i in reversed(range(cells)):
            value = forward[d, i] if i == 1 else forward[d, i] * inverse(d, i)
            if two is not None:
                value = value - kind(d, 4, i) * two
            if one is not None:
                value = value - kind(d, 3, i) * one
            whole[pl.ds(d * cells + i, fields, stride=total), :] = value
            one, two = value, one
    increment = mix(right, [whole[g * total : (g + 1) * total, :] for g in range(fields)])
    squares = sum(v * v for v in increment[1:]) + increment[0] * increment[0]
    squares = jnp.broadcast_to(jnp.sum(squares, axis=0, keepdims=True), (back - fields * cells, LANES))
    for d in range(parts):
        for f in range(fields):
            at = d * back + f * cells
            out[at : at + cells, :] = increment[f][d * cells : (d + 1) * cells, :]
        out[d * back + fields * cells : (d + 1) * back, :] = squares


def slab_kernel(peers, me, adj, grad, ctrl, *outs):
    fields, cells, length = adj.shape
    height = outs[0].shape[0]
    contribution = adj[0] * grad[0]
    for f in range(1, fields):
        contribution = contribution + adj[f] * grad[f]
    upper = contribution.astype(jnp.bfloat16).astype(jnp.float32)
    lower = contribution - upper
    high = lax.shift_right_logical(ctrl[...], 7)
    low = lax.bitwise_and(ctrl[...], LANES - 1)
    block = lax.broadcasted_iota(jnp.int32, (height, length), 0)
    lane = lax.broadcasted_iota(jnp.int32, (LANES, length), 0)
    sums = None
    for i in range(cells):
        hit = lane == low[i : i + 1, :]
        terms = jnp.concatenate(
            [
                jnp.where(hit, upper[i : i + 1, :], 0.0).astype(jnp.bfloat16),
                jnp.where(hit, lower[i : i + 1, :], 0.0).astype(jnp.bfloat16),
            ],
            axis=0,
        )
        rows = []
        for k in range(peers):
            offset = lax.bitwise_xor(me[0], k) * height
            rows.append(jnp.where(block == high[i : i + 1, :] - offset, 1.0, 0.0).astype(jnp.bfloat16))
        picked = jnp.concatenate(rows, axis=0)
        part = lax.dot_general(
            picked, terms, (((1,), (1,)), ((), ())), preferred_element_type=jnp.float32
        )
        sums = part if sums is None else sums + part
    sums = sums[:, :LANES] + sums[:, LANES:]
    for k in range(peers):
        outs[k][...] = sums[k * height : (k + 1) * height, :]


def finish_kernel(parts, width, peers, cell_count, adj, moved, *refs):
    squares, blocks, (out, sens) = refs[:peers], refs[peers : 2 * peers], refs[2 * peers :]
    fields, cells, _ = adj.shape
    back = moved.shape[0] // parts
    total = squares[0][...]
    slab = blocks[0][...]
    for k in range(1, peers):
        total = total + squares[k][...]
        slab = slab + blocks[k][...]
    sens[...] = slab
    total = jnp.sum(jnp.sum(total, axis=0, keepdims=True), axis=1, keepdims=True)
    factor = step_scale / jnp.sqrt(total / cell_count + epsilon)
    for d in range(parts):
        lanes = slice(d * width, (d + 1) * width)
        for f in range(fields):
            at = d * back + f * cells
            out[f, :, lanes] = adj[f, :, lanes] + factor * moved[at : at + cells, 0:width]


def shards(
    adjoint, source, shape_grad, lower_band, upper_band, jacobian, left_vectors, right_vectors, ctrl_local
):
    fields, cells, length = adjoint.shape
    parts, peers = lax.axis_size("stream"), lax.axis_size("cross")
    width = length // parts
    rows = block_rows(fields, cells)
    back = round_up(fields * cells + 1, SUBLANES)
    f32 = jnp.float32

    packed = pl.pallas_call(
        functools.partial(pack_kernel, parts, width),
        out_shape=pltpu.VMEM((parts, rows, LANES), f32),
        in_specs=[SMEM, SMEM, VMEM, VMEM, VMEM, VMEM],
        out_specs=VMEM,
        scratch_shapes=[pltpu.VMEM((fields, round_up(cells + 2, SUBLANES), length), f32)],
        name="pack",
    )(jacobian, left_vectors, adjoint, source, lower_band, upper_band)
    lines = lax.all_to_all(
        packed.reshape(parts * rows, LANES), "stream", split_axis=0, concat_axis=0, tiled=True
    )

    height = NCTRL // (parts * peers * LANES)
    me = lax.axis_index("cross").astype(jnp.int32).reshape(1)
    blocks = pl.pallas_call(
        functools.partial(slab_kernel, peers),
        out_shape=[pltpu.VMEM((height, LANES), f32)] * peers,
        in_specs=[SMEM, VMEM, VMEM, VMEM],
        out_specs=[VMEM] * peers,
        cost_estimate=pl.CostEstimate(
            flops=4 * cells * length * NCTRL // parts, bytes_accessed=4 << 20, transcendentals=0
        ),
        name="slab",
    )(me, adjoint, shape_grad, ctrl_local)

    def exchange(arrays):
        return [arrays[0]] + [
            lax.ppermute(arrays[k], "cross", [(i, i ^ k) for i in range(peers)])
            for k in range(1, peers)
        ]

    blocks = exchange(blocks)
    lines, *blocks = lax.optimization_barrier((lines, *blocks))

    moved = pl.pallas_call(
        functools.partial(solve_kernel, parts, fields, cells),
        out_shape=pltpu.VMEM((parts * back, LANES), f32),
        in_specs=[SMEM, SMEM, SMEM, VMEM],
        out_specs=VMEM,
        scratch_shapes=[
            pltpu.VMEM((2 * fields * parts, LANES), f32),
            pltpu.VMEM((fields * parts * cells, LANES), f32),
        ],
        name="solve",
    )(jacobian, left_vectors, right_vectors, held(lines))
    moved = lax.all_to_all(moved, "stream", split_axis=0, concat_axis=0, tiled=True)
    squares = moved.reshape(parts, back, LANES)[:, fields * cells, :]
    squares = exchange([squares] * peers)

    cell_count = fields * cells * length * parts * peers
    adjoint_next, sensitivity = pl.pallas_call(
        functools.partial(finish_kernel, parts, width, peers, cell_count),
        out_shape=[
            jax.ShapeDtypeStruct(adjoint.shape, f32),
            jax.ShapeDtypeStruct((height, LANES), f32),
        ],
        in_specs=[VMEM] * (2 + 2 * peers),
        out_specs=[VMEM, VMEM],
        name="finish",
    )(adjoint, *(held(a) for a in (moved, *squares, *blocks)))
    return adjoint_next, sensitivity.reshape(height * LANES)


def solution(mesh):
    in_specs = (
        P(None, "stream", "cross"),
        P(None, "stream", "cross"),
        P(None, "stream", "cross"),
        P(None, None, "stream", "cross"),
        P(None, None, "stream", "cross"),
        P(),
        P(),
        P(),
        P("stream", "cross"),
    )
    out_specs = (P(None, "stream", "cross"), P(("stream", "cross")))
    return jax.shard_map(shards, mesh=mesh, in_specs=in_specs, out_specs=out_specs, check_vma=False)
```

```python
import functools

import jax
import jax.numpy as jnp
from jax import lax
from jax.experimental import pallas as pl
from jax.experimental.pallas import tpu as pltpu
from jax.sharding import PartitionSpec as P

NCTRL = 524288
LANES = 128
SUBLANES = 8

dissipation = 0.25
step_scale = 0.5
epsilon = 1e-06

VMEM = pl.BlockSpec(memory_space=pltpu.VMEM)
SMEM = pl.BlockSpec(memory_space=pltpu.SMEM)


def held(array):
    return pltpu.with_memory_space_constraint(array, pltpu.VMEM)


def round_up(value, step):
    return -(-value // step) * step


def mix(matrix_ref, columns):
    count = len(columns)
    return [
        sum(matrix_ref[f, g] * columns[g] for g in range(1, count)) + matrix_ref[f, 0] * columns[0]
        for f in range(count)
    ]


CELL_KINDS = 5


def block_rows(fields, cells):
    return round_up(fields * (CELL_KINDS * cells + cells - 1 + 2), SUBLANES)


def spread(scratch, me, outs):
    for k, out in enumerate(outs):
        out[...] = scratch[lax.bitwise_xor(me[0], k)]


def pack_kernel(group, width, me, jac, left, adj, src, low, up, *refs):
    outs, (blocks, pad) = refs[:group], refs[group:]
    fields, cells, length = adj.shape
    rows = block_rows(fields, cells)
    if width < LANES or rows > fields * (CELL_KINDS * cells + cells + 1):
        blocks[...] = jnp.zeros_like(blocks)
    pad[...] = jnp.zeros_like(pad)
    for f in range(fields):
        pad[f, 1 : cells + 1, :] = adj[f]
    ahead = [pad[f, 2 : cells + 2, :] for f in range(fields)]
    behind = [pad[f, 0:cells, :] for f in range(fields)]
    central = mix(jac, [a - b for a, b in zip(ahead, behind)])
    residual = [
        src[f] - 0.5 * central[f] + dissipation * (ahead[f] - 2.0 * adj[f] + behind[f])
        for f in range(fields)
    ]
    characteristic = mix(left, residual)
    cell = lax.broadcasted_iota(jnp.int32, (cells, length), 0)
    extra = CELL_KINDS * fields * cells
    for f in range(fields):
        diagonal = up[0, f]
        inverse = 1.0 / diagonal
        own = jnp.where(cell == 1, inverse, 1.0)
        diagonal_1 = jnp.broadcast_to(up[0, f, 1:2, :], (cells, length))
        values = (
            characteristic[f] * own,
            low[0, f] * jnp.where(cell == 2, diagonal_1, own),
            low[1, f] * jnp.where(cell == 3, diagonal_1, own),
            up[1, f] * inverse,
            up[2, f] * inverse,
        )
        for d, base, lanes, to in pieces(group, width, rows):
            for k, value in enumerate(values):
                at = base + (k * fields + f) * cells
                blocks[d, at : at + cells, to] = value[:, lanes]
            at = base + extra + f * (cells + 1)
            blocks[d, at : at + 1, to] = inverse[0:1, lanes]
            blocks[d, at + 1 : at + cells - 1, to] = inverse[2:cells, lanes]
            blocks[d, at + cells - 1 : at + cells, to] = adj[f, 0:1, lanes]
            blocks[d, at + cells : at + cells + 1, to] = adj[f, cells - 1 : cells, lanes]
    spread(blocks, me, outs)


def pieces(group, width, rows):
    step = min(width, LANES)
    for d in range(group):
        for b in range(width // step):
            start = d * width + b * step
            yield d, b * rows, slice(start, start + step), slice(0, step)


class Lines:
    def __init__(self, ref, fields, cells, base):
        self.ref, self.fields, self.cells, self.base = ref, fields, cells, base

    def value(self, d, k, i):
        at = self.base(d) + k * self.fields * self.cells + i
        return self.ref[pl.ds(at, self.fields, stride=self.cells), :]

    def divided(self, d, i, value):
        if i == 1:
            return value
        at = self.base(d) + CELL_KINDS * self.fields * self.cells + (i if i == 0 else i - 1)
        return value * self.ref[pl.ds(at, self.fields, stride=self.cells + 1), :]


def less(value, factor, other):
    if other is None:
        return value
    return -(factor * other) if value is None else value - factor * other


SLOTS = 8


def sweep_kernel(group, fields, cells, me, half, jac, left, *refs):
    received, (lines, edge, message) = refs[:group], refs[group:]
    rows = block_rows(fields, cells)
    size = received[0].shape[0]
    count = size // rows
    for k in range(group):
        at = pl.multiple_of(lax.bitwise_xor(me[0], k) * size, SUBLANES)
        lines[pl.ds(at, size), :] = received[k][...]
    lower_half = jnp.full((fields, LANES), half[0], jnp.int32) == 0
    extra = CELL_KINDS * fields * cells
    for b in range(count):

        def across(row):
            return lines[pl.ds(b * rows + row, group, stride=size), :]

        firsts = [across(extra + f * (cells + 1) + cells - 1) for f in range(fields)]
        lasts = [across(extra + f * (cells + 1) + cells) for f in range(fields)]
        from_last = mix(jac, lasts)
        from_first = mix(jac, firsts)
        into_first = mix(left, [0.5 * x + dissipation * y for x, y in zip(from_last, lasts)])
        into_last = mix(left, [dissipation * y - 0.5 * x for x, y in zip(from_first, firsts)])
        at = 2 * b * fields * group
        for f in range(fields):
            edge[at + f * group : at + (f + 1) * group, :] = into_first[f]
            edge[at + (fields + f) * group : at + (fields + f + 1) * group, :] = into_last[f]

        def to_next(d):
            return edge[pl.ds(at + d, fields, stride=group), :]

        def to_previous(d):
            return edge[pl.ds(at + fields * group + d, fields, stride=group), :]

        view = Lines(lines, fields, cells, lambda d: (d * count + b) * rows)
        ones = jnp.ones((fields, LANES), jnp.float32)
        one, two = [None, ones, None], [None, None, None]
        forward = {}
        for d in range(group):
            for i in range(cells):
                value = view.value(d, 0, i)
                if i == 0 and d > 0:
                    value = value + to_next(d - 1)
                if i == cells - 1 and d < group - 1:
                    value = value + to_previous(d + 1)
                start = [value, None, ones if d == 0 and i == 0 else None]
                first, second = view.value(d, 1, i), view.value(d, 2, i)
                now = [less(less(start[c], second, two[c]), first, one[c]) for c in range(3)]
                forward[d, i] = now
                one, two = now, one
        ends = [one[0], two[0], to_next(group - 1)]
        one, two = [None] * 3, [None] * 3
        for d in reversed(range(group)):
            for i in reversed(range(cells)):
                start = [view.divided(d, i, value) for value in forward[d, i]]
                first, second = view.value(d, 3, i), view.value(d, 4, i)
                now = [less(less(start[c], second, two[c]), first, one[c]) for c in range(3)]
                one, two = now, one
        begins = [one[0], two[0], to_previous(0)]
        slots = [jnp.where(lower_half, x, y) for x, y in zip(ends, begins)]
        slots += [one[1], two[1], one[2], two[2], view.value(0, 2, 0)]
        for k, value in enumerate(slots):
            row = (b * SLOTS + k) * fields
            message[row : row + fields, :] = value


def solve_kernel(group, fields, cells, me, half, right, lines, edge, mine, other, *refs):
    outs, (squares, whole, blocks) = refs[:group], refs[group:]
    rows = block_rows(fields, cells)
    size = lines.shape[0] // group
    count = size // rows
    total = group * cells
    lower_half = jnp.full((fields, LANES), half[0], jnp.int32) == 0
    summed = None
    for b in range(count):
        view = Lines(lines, fields, cells, lambda d: (d * count + b) * rows)
        at = 2 * b * fields * group

        def to_next(d):
            return edge[pl.ds(at + d, fields, stride=group), :]

        def to_previous(d):
            return edge[pl.ds(at + fields * group + d, fields, stride=group), :]

        def slot(ref, k):
            row = (b * SLOTS + k) * fields
            return ref[row : row + fields, :]

        def of_lower(k):
            return jnp.where(lower_half, slot(mine, k), slot(other, k))

        def of_upper(k):
            return jnp.where(lower_half, slot(other, k), slot(mine, k))

        zeros = jnp.zeros((fields, LANES), jnp.float32)
        onto_last, onto_first = of_upper(2), of_lower(2)
        before, before_2 = of_lower(0) + onto_last, of_lower(1)
        added = onto_first - of_upper(7) * before_2
        after = of_upper(0) + of_upper(3) * before + of_upper(5) * added
        after_2 = of_upper(1) + of_upper(4) * before + of_upper(6) * added
        one, two = jnp.where(lower_half, zeros, before), jnp.where(lower_half, zeros, before_2)
        onto_first = jnp.where(lower_half, zeros, onto_first)
        onto_last = jnp.where(lower_half, onto_last, zeros)
        forward = {}
        for d in range(group):
            for i in range(cells):
                value = view.value(d, 0, i)
                if i == 0:
                    value = value + (to_next(d - 1) if d > 0 else onto_first)
                if i == cells - 1:
                    value = value + (to_previous(d + 1) if d < group - 1 else onto_last)
                value = less(less(value, view.value(d, 2, i), two), view.value(d, 1, i), one)
                forward[d, i] = value
                one, two = value, one
        one, two = jnp.where(lower_half, after, zeros), jnp.where(lower_half, after_2, zeros)
        for d in reversed(range(group)):
            for i in reversed(range(cells)):
                value = view.divided(d, i, forward[d, i])
                value = less(less(value, view.value(d, 4, i), two), view.value(d, 3, i), one)
                whole[pl.ds(b * fields * total + d * cells + i, fields, stride=total), :] = value
                one, two = value, one
        columns = [(b * fields + g) * total for g in range(fields)]
        increment = mix(right, [whole[at : at + total, :] for at in columns])
        for f in range(fields):
            part = jnp.sum(increment[f] * increment[f], axis=0, keepdims=True)
            summed = part if summed is None else summed + part
            for d in range(group):
                row = (b * fields + f) * cells
                blocks[d, row : row + cells, :] = increment[f][d * cells : (d + 1) * cells, :]
    spread(blocks, me, outs)
    for n in range(squares.shape[0]):
        squares[n] = summed


def slab_kernel(peers, me, adj, grad, ctrl, *outs):
    fields, cells, length = adj.shape
    height = outs[0].shape[0]
    contribution = adj[0] * grad[0]
    for f in range(1, fields):
        contribution = contribution + adj[f] * grad[f]
    upper = contribution.astype(jnp.bfloat16).astype(jnp.float32)
    lower = contribution - upper
    high = lax.shift_right_logical(ctrl[...], 7)
    low = lax.bitwise_and(ctrl[...], LANES - 1)
    block = lax.broadcasted_iota(jnp.int32, (height, length), 0)
    lane = lax.broadcasted_iota(jnp.int32, (LANES, length), 0)
    sums = None
    for i in range(cells):
        hit = lane == low[i : i + 1, :]
        terms = jnp.concatenate(
            [
                jnp.where(hit, upper[i : i + 1, :], 0.0).astype(jnp.bfloat16),
                jnp.where(hit, lower[i : i + 1, :], 0.0).astype(jnp.bfloat16),
            ],
            axis=0,
        )
        rows = []
        for k in range(peers):
            offset = lax.bitwise_xor(me[0], k) * height
            rows.append(jnp.where(block == high[i : i + 1, :] - offset, 1.0, 0.0).astype(jnp.bfloat16))
        picked = jnp.concatenate(rows, axis=0)
        part = lax.dot_general(
            picked, terms, (((1,), (1,)), ((), ())), preferred_element_type=jnp.float32
        )
        sums = part if sums is None else sums + part
    sums = sums[:, :LANES] + sums[:, LANES:]
    for k in range(peers):
        outs[k][...] = sums[k * height : (k + 1) * height, :]


def finish_kernel(group, width, peers, cell_count, me, adj, squares, *refs):
    moved, slabs, (out, sens, blocks) = refs[:group], refs[group : group + peers], refs[group + peers :]
    fields, cells, _ = adj.shape
    for k in range(group):
        blocks[lax.bitwise_xor(me[0], k)] = moved[k][...]
    slab = slabs[0][...]
    for k in range(1, peers):
        slab = slab + slabs[k][...]
    sens[...] = slab
    total = jnp.sum(jnp.sum(squares[...], axis=0), axis=1, keepdims=True)
    factor = step_scale / jnp.sqrt(total / cell_count + epsilon)
    for d, base, lanes, to in pieces(group, width, fields * cells):
        for f in range(fields):
            at = base + f * cells
            out[f, :, lanes] = adj[f, :, lanes] + factor * blocks[d, at : at + cells, to]


def swap(array, axis, k):
    return lax.ppermute(array, axis, [(i, i ^ k) for i in range(lax.axis_size(axis))])


def exchange(arrays, axis):
    return [arrays[0]] + [swap(arrays[k], axis, k) for k in range(1, len(arrays))]


def shards(
    adjoint, source, shape_grad, lower_band, upper_band, jacobian, left_vectors, right_vectors, ctrl_local
):
    fields, cells, length = adjoint.shape
    parts, peers = lax.axis_size("stream"), lax.axis_size("cross")
    group = parts // 2
    width = length // group
    count = -(-width // LANES)
    rows = count * block_rows(fields, cells)
    back = count * fields * cells
    f32 = jnp.float32

    at = lax.axis_index("stream").astype(jnp.int32)
    me, half = (at % group).reshape(1), (at // group).reshape(1)
    packed = pl.pallas_call(
        functools.partial(pack_kernel, group, width),
        out_shape=[pltpu.VMEM((rows, LANES), f32)] * group,
        in_specs=[SMEM, SMEM, SMEM, VMEM, VMEM, VMEM, VMEM],
        out_specs=[VMEM] * group,
        scratch_shapes=[
            pltpu.VMEM((group, rows, LANES), f32),
            pltpu.VMEM((fields, round_up(cells + 2, SUBLANES), length), f32),
        ],
        name="pack",
    )(me, jacobian, left_vectors, adjoint, source, lower_band, upper_band)
    received = exchange(packed, "stream")

    height = NCTRL // (parts * peers * LANES)
    column = lax.axis_index("cross").astype(jnp.int32).reshape(1)
    slabs = pl.pallas_call(
        functools.partial(slab_kernel, peers),
        out_shape=[pltpu.VMEM((height, LANES), f32)] * peers,
        in_specs=[SMEM, VMEM, VMEM, VMEM],
        out_specs=[VMEM] * peers,
        cost_estimate=pl.CostEstimate(
            flops=4 * cells * length * NCTRL // parts, bytes_accessed=4 << 20, transcendentals=0
        ),
        name="slab",
    )(column, adjoint, shape_grad, ctrl_local)
    *received, slabs = lax.optimization_barrier((*received, slabs))

    lines, edge, message = pl.pallas_call(
        functools.partial(sweep_kernel, group, fields, cells),
        out_shape=[
            pltpu.VMEM((group * rows, LANES), f32),
            pltpu.VMEM((2 * count * fields * group, LANES), f32),
            pltpu.VMEM((count * SLOTS * fields, LANES), f32),
        ],
        in_specs=[SMEM] * 4 + [VMEM] * group,
        out_specs=[VMEM] * 3,
        name="sweep",
    )(me, half, jacobian, left_vectors, *(held(a) for a in received))
    other = swap(message, "stream", group)
    slabs = exchange(slabs, "cross")
    other, *slabs = lax.optimization_barrier((other, *slabs))

    *moved, squares = pl.pallas_call(
        functools.partial(solve_kernel, group, fields, cells),
        out_shape=[pltpu.VMEM((back, LANES), f32)] * group
        + [pltpu.VMEM((parts * peers, 1, LANES), f32)],
        in_specs=[SMEM] * 3 + [VMEM] * 4,
        out_specs=[VMEM] * (group + 1),
        scratch_shapes=[
            pltpu.VMEM((count * fields * group * cells, LANES), f32),
            pltpu.VMEM((group, back, LANES), f32),
        ],
        name="solve",
    )(me, half, right_vectors, *(held(a) for a in (lines, edge, message, other)))
    squares = lax.all_to_all(squares, ("stream", "cross"), split_axis=0, concat_axis=0, tiled=True)
    moved = exchange(moved, "stream")

    cell_count = fields * cells * length * parts * peers
    adjoint_next, sensitivity = pl.pallas_call(
        functools.partial(finish_kernel, group, width, peers, cell_count),
        out_shape=[
            jax.ShapeDtypeStruct(adjoint.shape, f32),
            jax.ShapeDtypeStruct((height, LANES), f32),
        ],
        in_specs=[SMEM] + [VMEM] * (2 + group + peers),
        out_specs=[VMEM, VMEM],
        scratch_shapes=[pltpu.VMEM((group, back, LANES), f32)],
        name="finish",
    )(me, adjoint, *(held(a) for a in (squares, *moved, *slabs)))
    return adjoint_next, sensitivity.reshape(height * LANES)


def solution(mesh):
    in_specs = (
        P(None, "stream", "cross"),
        P(None, "stream", "cross"),
        P(None, "stream", "cross"),
        P(None, None, "stream", "cross"),
        P(None, None, "stream", "cross"),
        P(),
        P(),
        P(),
        P("stream", "cross"),
    )
    out_specs = (P(None, "stream", "cross"), P(("stream", "cross")))
    return jax.shard_map(shards, mesh=mesh, in_specs=in_specs, out_specs=out_specs, check_vma=False)
```

```python
import functools

import jax
import jax.numpy as jnp
from jax import lax
from jax.experimental import pallas as pl
from jax.experimental.pallas import tpu as pltpu
from jax.sharding import PartitionSpec as P

NCTRL = 524288
LANES = 128
SUBLANES = 8

dissipation = 0.25
step_scale = 0.5
epsilon = 1e-06

VMEM = pl.BlockSpec(memory_space=pltpu.VMEM)
SMEM = pl.BlockSpec(memory_space=pltpu.SMEM)


def held(array):
    return pltpu.with_memory_space_constraint(array, pltpu.VMEM)


def round_up(value, step):
    return -(-value // step) * step


def mix(matrix_ref, columns):
    count = len(columns)
    return [
        sum(matrix_ref[f, g] * columns[g] for g in range(1, count)) + matrix_ref[f, 0] * columns[0]
        for f in range(count)
    ]


CELL_KINDS = 5


def block_rows(fields, cells):
    return round_up(fields * (CELL_KINDS * cells + cells - 1 + 2), SUBLANES)


def spread(scratch, me, outs):
    for k, out in enumerate(outs):
        out[...] = scratch[lax.bitwise_xor(me[0], k)]


def pack_kernel(group, width, me, jac, left, adj, src, low, up, *refs):
    outs, (blocks, pad) = refs[:group], refs[group:]
    fields, cells, length = adj.shape
    rows = block_rows(fields, cells)
    if width < LANES or rows > fields * (CELL_KINDS * cells + cells + 1):
        blocks[...] = jnp.zeros_like(blocks)
    pad[...] = jnp.zeros_like(pad)
    for f in range(fields):
        pad[f, 1 : cells + 1, :] = adj[f]
    ahead = [pad[f, 2 : cells + 2, :] for f in range(fields)]
    behind = [pad[f, 0:cells, :] for f in range(fields)]
    central = mix(jac, [a - b for a, b in zip(ahead, behind)])
    residual = [
        src[f] - 0.5 * central[f] + dissipation * (ahead[f] - 2.0 * adj[f] + behind[f])
        for f in range(fields)
    ]
    characteristic = mix(left, residual)
    cell = lax.broadcasted_iota(jnp.int32, (cells, length), 0)
    extra = CELL_KINDS * fields * cells
    for f in range(fields):
        diagonal = up[0, f]
        inverse = 1.0 / diagonal
        own = jnp.where(cell == 1, inverse, 1.0)
        diagonal_1 = jnp.broadcast_to(up[0, f, 1:2, :], (cells, length))
        values = (
            characteristic[f] * own,
            low[0, f] * jnp.where(cell == 2, diagonal_1, own),
            low[1, f] * jnp.where(cell == 3, diagonal_1, own),
            up[1, f] * inverse,
            up[2, f] * inverse,
        )
        for d, base, lanes, to in pieces(group, width, rows):
            for k, value in enumerate(values):
                at = base + (k * fields + f) * cells
                blocks[d, at : at + cells, to] = value[:, lanes]
            at = base + extra + f * (cells + 1)
            blocks[d, at : at + 1, to] = inverse[0:1, lanes]
            blocks[d, at + 1 : at + cells - 1, to] = inverse[2:cells, lanes]
            blocks[d, at + cells - 1 : at + cells, to] = adj[f, 0:1, lanes]
            blocks[d, at + cells : at + cells + 1, to] = adj[f, cells - 1 : cells, lanes]
    spread(blocks, me, outs)


def pieces(group, width, rows):
    step = min(width, LANES)
    for d in range(group):
        for b in range(width // step):
            start = d * width + b * step
            yield d, b * rows, slice(start, start + step), slice(0, step)


class Lines:
    def __init__(self, ref, fields, cells, base):
        self.ref, self.fields, self.cells, self.base = ref, fields, cells, base

    def value(self, d, k, i):
        at = self.base(d) + k * self.fields * self.cells + i
        return self.ref[pl.ds(at, self.fields, stride=self.cells), :]

    def divided(self, d, i, value):
        if i == 1:
            return value
        at = self.base(d) + CELL_KINDS * self.fields * self.cells + (i if i == 0 else i - 1)
        return value * self.ref[pl.ds(at, self.fields, stride=self.cells + 1), :]


def less(value, factor, other):
    if other is None:
        return value
    return -(factor * other) if value is None else value - factor * other


SLOTS = 8


def sweep_kernel(group, fields, cells, me, half, jac, left, *refs):
    received, (lines, edge, message) = refs[:group], refs[group:]
    rows = block_rows(fields, cells)
    size = received[0].shape[0]
    count = size // rows
    for k in range(group):
        at = pl.multiple_of(lax.bitwise_xor(me[0], k) * size, SUBLANES)
        lines[pl.ds(at, size), :] = received[k][...]
    lower_half = jnp.full((fields, LANES), half[0], jnp.int32) == 0
    extra = CELL_KINDS * fields * cells
    for b in range(count):

        def across(row):
            return lines[pl.ds(b * rows + row, group, stride=size), :]

        firsts = [across(extra + f * (cells + 1) + cells - 1) for f in range(fields)]
        lasts = [across(extra + f * (cells + 1) + cells) for f in range(fields)]
        from_last = mix(jac, lasts)
        from_first = mix(jac, firsts)
        into_first = mix(left, [0.5 * x + dissipation * y for x, y in zip(from_last, lasts)])
        into_last = mix(left, [dissipation * y - 0.5 * x for x, y in zip(from_first, firsts)])
        at = 2 * b * fields * group
        for f in range(fields):
            edge[at + f * group : at + (f + 1) * group, :] = into_first[f]
            edge[at + (fields + f) * group : at + (fields + f + 1) * group, :] = into_last[f]

        def to_next(d):
            return edge[pl.ds(at + d, fields, stride=group), :]

        def to_previous(d):
            return edge[pl.ds(at + fields * group + d, fields, stride=group), :]

        view = Lines(lines, fields, cells, lambda d: (d * count + b) * rows)
        ones = jnp.ones((fields, LANES), jnp.float32)
        one, two = [None, ones, None], [None, None, None]
        forward = {}
        for d in range(group):
            for i in range(cells):
                value = view.value(d, 0, i)
                if i == 0 and d > 0:
                    value = value + to_next(d - 1)
                if i == cells - 1 and d < group - 1:
                    value = value + to_previous(d + 1)
                start = [value, None, ones if d == 0 and i == 0 else None]
                first, second = view.value(d, 1, i), view.value(d, 2, i)
                now = [less(less(start[c], second, two[c]), first, one[c]) for c in range(3)]
                forward[d, i] = now
                one, two = now, one
        ends = [one[0], two[0], to_next(group - 1)]
        one, two = [None] * 3, [None] * 3
        for d in reversed(range(group)):
            for i in reversed(range(cells)):
                start = [view.divided(d, i, value) for value in forward[d, i]]
                first, second = view.value(d, 3, i), view.value(d, 4, i)
                now = [less(less(start[c], second, two[c]), first, one[c]) for c in range(3)]
                one, two = now, one
        begins = [one[0], two[0], to_previous(0)]
        slots = [jnp.where(lower_half, x, y) for x, y in zip(ends, begins)]
        slots += [one[1], two[1], one[2], two[2], view.value(0, 2, 0)]
        for k, value in enumerate(slots):
            row = (b * SLOTS + k) * fields
            message[row : row + fields, :] = value


def solve_kernel(group, fields, cells, me, half, right, lines, edge, mine, other, *refs):
    outs, (squares, whole, blocks) = refs[:group], refs[group:]
    rows = block_rows(fields, cells)
    size = lines.shape[0] // group
    count = size // rows
    total = group * cells
    lower_half = jnp.full((fields, LANES), half[0], jnp.int32) == 0
    summed = None
    for b in range(count):
        view = Lines(lines, fields, cells, lambda d: (d * count + b) * rows)
        at = 2 * b * fields * group

        def to_next(d):
            return edge[pl.ds(at + d, fields, stride=group), :]

        def to_previous(d):
            return edge[pl.ds(at + fields * group + d, fields, stride=group), :]

        def slot(ref, k):
            row = (b * SLOTS + k) * fields
            return ref[row : row + fields, :]

        def of_lower(k):
            return jnp.where(lower_half, slot(mine, k), slot(other, k))

        def of_upper(k):
            return jnp.where(lower_half, slot(other, k), slot(mine, k))

        zeros = jnp.zeros((fields, LANES), jnp.float32)
        onto_last, onto_first = of_upper(2), of_lower(2)
        before, before_2 = of_lower(0) + onto_last, of_lower(1)
        added = onto_first - of_upper(7) * before_2
        after = of_upper(0) + of_upper(3) * before + of_upper(5) * added
        after_2 = of_upper(1) + of_upper(4) * before + of_upper(6) * added
        one, two = jnp.where(lower_half, zeros, before), jnp.where(lower_half, zeros, before_2)
        onto_first = jnp.where(lower_half, zeros, onto_first)
        onto_last = jnp.where(lower_half, onto_last, zeros)
        forward = {}
        for d in range(group):
            for i in range(cells):
                value = view.value(d, 0, i)
                if i == 0:
                    value = value + (to_next(d - 1) if d > 0 else onto_first)
                if i == cells - 1:
                    value = value + (to_previous(d + 1) if d < group - 1 else onto_last)
                value = less(less(value, view.value(d, 2, i), two), view.value(d, 1, i), one)
                forward[d, i] = value
                one, two = value, one
        one, two = jnp.where(lower_half, after, zeros), jnp.where(lower_half, after_2, zeros)
        for d in reversed(range(group)):
            for i in reversed(range(cells)):
                value = view.divided(d, i, forward[d, i])
                value = less(less(value, view.value(d, 4, i), two), view.value(d, 3, i), one)
                whole[pl.ds(b * fields * total + d * cells + i, fields, stride=total), :] = value
                one, two = value, one
        columns = [(b * fields + g) * total for g in range(fields)]
        increment = mix(right, [whole[at : at + total, :] for at in columns])
        for f in range(fields):
            part = jnp.sum(increment[f] * increment[f], axis=0, keepdims=True)
            summed = part if summed is None else summed + part
            for d in range(group):
                row = (b * fields + f) * cells
                blocks[d, row : row + cells, :] = increment[f][d * cells : (d + 1) * cells, :]
    spread(blocks, me, outs)
    for n in range(squares.shape[0]):
        squares[n] = summed


def slab_kernel(peers, me, adj, grad, ctrl, *outs):
    fields, cells, length = adj.shape
    height = outs[0].shape[0]
    contribution = adj[0] * grad[0]
    for f in range(1, fields):
        contribution = contribution + adj[f] * grad[f]
    upper = contribution.astype(jnp.bfloat16).astype(jnp.float32)
    lower = contribution - upper
    high = lax.shift_right_logical(ctrl[...], 7)
    low = lax.bitwise_and(ctrl[...], LANES - 1)
    block = lax.broadcasted_iota(jnp.int32, (height, length), 0)
    lane = lax.broadcasted_iota(jnp.int32, (LANES, length), 0)
    sums = None
    for i in range(cells):
        hit = lane == low[i : i + 1, :]
        terms = jnp.concatenate(
            [
                jnp.where(hit, upper[i : i + 1, :], 0.0).astype(jnp.bfloat16),
                jnp.where(hit, lower[i : i + 1, :], 0.0).astype(jnp.bfloat16),
            ],
            axis=0,
        )
        rows = []
        for k in range(peers):
            offset = lax.bitwise_xor(me[0], k) * height
            rows.append(jnp.where(block == high[i : i + 1, :] - offset, 1.0, 0.0).astype(jnp.bfloat16))
        picked = jnp.concatenate(rows, axis=0)
        part = lax.dot_general(
            picked, terms, (((1,), (1,)), ((), ())), preferred_element_type=jnp.float32
        )
        sums = part if sums is None else sums + part
    sums = sums[:, :LANES] + sums[:, LANES:]
    for k in range(peers):
        outs[k][...] = sums[k * height : (k + 1) * height, :]


def finish_kernel(group, width, peers, cell_count, me, adj, squares, *refs):
    moved, slabs, (out, sens, blocks) = refs[:group], refs[group : group + peers], refs[group + peers :]
    fields, cells, _ = adj.shape
    for k in range(group):
        blocks[lax.bitwise_xor(me[0], k)] = moved[k][...]
    slab = slabs[0][...]
    for k in range(1, peers):
        slab = slab + slabs[k][...]
    sens[...] = slab
    total = jnp.sum(jnp.sum(squares[...], axis=0), axis=1, keepdims=True)
    factor = step_scale / jnp.sqrt(total / cell_count + epsilon)
    for d, base, lanes, to in pieces(group, width, fields * cells):
        for f in range(fields):
            at = base + f * cells
            out[f, :, lanes] = adj[f, :, lanes] + factor * blocks[d, at : at + cells, to]


def swap(array, axis, k):
    return lax.ppermute(array, axis, [(i, i ^ k) for i in range(lax.axis_size(axis))])


def exchange(arrays, axis):
    return [arrays[0]] + [swap(arrays[k], axis, k) for k in range(1, len(arrays))]


def shards(
    adjoint, source, shape_grad, lower_band, upper_band, jacobian, left_vectors, right_vectors, ctrl_local
):
    fields, cells, length = adjoint.shape
    parts, peers = lax.axis_size("stream"), lax.axis_size("cross")
    group = parts // 2
    width = length // group
    count = -(-width // LANES)
    rows = count * block_rows(fields, cells)
    back = count * fields * cells
    f32 = jnp.float32

    at = lax.axis_index("stream").astype(jnp.int32)
    me, half = lax.rem(at, group).reshape(1), lax.div(at, group).reshape(1)
    packed = pl.pallas_call(
        functools.partial(pack_kernel, group, width),
        out_shape=[pltpu.VMEM((rows, LANES), f32)] * group,
        in_specs=[SMEM, SMEM, SMEM, VMEM, VMEM, VMEM, VMEM],
        out_specs=[VMEM] * group,
        scratch_shapes=[
            pltpu.VMEM((group, rows, LANES), f32),
            pltpu.VMEM((fields, round_up(cells + 2, SUBLANES), length), f32),
        ],
        name="pack",
    )(me, jacobian, left_vectors, adjoint, source, lower_band, upper_band)
    received = exchange(packed, "stream")

    height = NCTRL // (parts * peers * LANES)
    column = lax.axis_index("cross").astype(jnp.int32).reshape(1)
    slabs = pl.pallas_call(
        functools.partial(slab_kernel, peers),
        out_shape=[pltpu.VMEM((height, LANES), f32)] * peers,
        in_specs=[SMEM, VMEM, VMEM, VMEM],
        out_specs=[VMEM] * peers,
        cost_estimate=pl.CostEstimate(
            flops=4 * cells * length * NCTRL // parts, bytes_accessed=4 << 20, transcendentals=0
        ),
        name="slab",
    )(column, adjoint, shape_grad, ctrl_local)
    *received, slabs = lax.optimization_barrier((*received, slabs))

    lines, edge, message = pl.pallas_call(
        functools.partial(sweep_kernel, group, fields, cells),
        out_shape=[
            pltpu.VMEM((group * rows, LANES), f32),
            pltpu.VMEM((2 * count * fields * group, LANES), f32),
            pltpu.VMEM((count * SLOTS * fields, LANES), f32),
        ],
        in_specs=[SMEM] * 4 + [VMEM] * group,
        out_specs=[VMEM] * 3,
        name="sweep",
    )(me, half, jacobian, left_vectors, *(held(a) for a in received))
    other = swap(message, "stream", group)
    slabs = exchange(slabs, "cross")

    *moved, squares = pl.pallas_call(
        functools.partial(solve_kernel, group, fields, cells),
        out_shape=[pltpu.VMEM((back, LANES), f32)] * group
        + [pltpu.VMEM((parts * peers, 1, LANES), f32)],
        in_specs=[SMEM] * 3 + [VMEM] * 4,
        out_specs=[VMEM] * (group + 1),
        scratch_shapes=[
            pltpu.VMEM((count * fields * group * cells, LANES), f32),
            pltpu.VMEM((group, back, LANES), f32),
        ],
        name="solve",
    )(me, half, right_vectors, *(held(a) for a in (lines, edge, message, other)))
    squares = lax.all_to_all(squares, ("stream", "cross"), split_axis=0, concat_axis=0, tiled=True)
    moved = exchange(moved, "stream")

    cell_count = fields * cells * length * parts * peers
    adjoint_next, sensitivity = pl.pallas_call(
        functools.partial(finish_kernel, group, width, peers, cell_count),
        out_shape=[
            jax.ShapeDtypeStruct(adjoint.shape, f32),
            jax.ShapeDtypeStruct((height, LANES), f32),
        ],
        in_specs=[SMEM] + [VMEM] * (2 + group + peers),
        out_specs=[VMEM, VMEM],
        scratch_shapes=[pltpu.VMEM((group, back, LANES), f32)],
        name="finish",
    )(me, adjoint, *(held(a) for a in (squares, *moved, *slabs)))
    return adjoint_next, sensitivity.reshape(height * LANES)


def solution(mesh):
    in_specs = (
        P(None, "stream", "cross"),
        P(None, "stream", "cross"),
        P(None, "stream", "cross"),
        P(None, None, "stream", "cross"),
        P(None, None, "stream", "cross"),
        P(),
        P(),
        P(),
        P("stream", "cross"),
    )
    out_specs = (P(None, "stream", "cross"), P(("stream", "cross")))
    return jax.shard_map(shards, mesh=mesh, in_specs=in_specs, out_specs=out_specs, check_vma=False)
```

```python
import functools

import jax
import jax.numpy as jnp
from jax import lax
from jax.experimental import pallas as pl
from jax.experimental.pallas import tpu as pltpu
from jax.sharding import PartitionSpec as P


NCTRL = 524288
LANES = 128
SUBLANES = 8

dissipation = 0.25
step_scale = 0.5
epsilon = 1e-06


VMEM = pl.BlockSpec(memory_space=pltpu.VMEM)
SMEM = pl.BlockSpec(memory_space=pltpu.SMEM)


def held(array):
    return pltpu.with_memory_space_constraint(array, pltpu.VMEM)


def round_up(value, step):
    return -(-value // step) * step


def mix(entry, columns):
    count = len(columns)
    return [
        sum(entry(f, g) * columns[g] for g in range(1, count)) + entry(f, 0) * columns[0]
        for f in range(count)
    ]


def scalars(matrix):
    return lambda f, g: matrix[f, g]


def table_rows(fields):
    return round_up(3 * fields * fields, SUBLANES)


def table_entries(table, fields, which):
    def entry(f, g):
        row = (which * fields + f) * fields + g
        return table[row : row + 1, :]

    return entry


CELL_KINDS = 5


def block_rows(fields, cells):
    return round_up(fields * (CELL_KINDS * cells + cells - 1 + 2), SUBLANES)


def spread(scratch, me, outs):
    for k, out in enumerate(outs):
        out[...] = scratch[lax.bitwise_xor(me[0], k)]


def pack_kernel(group, width, me, jac, left, right, adj, src, low, up, *refs):
    outs, (table, blocks, pad) = refs[:group], refs[group:]
    fields, cells, length = adj.shape
    for which, matrix in enumerate((jac, left, right)):
        for f in range(fields):
            for g in range(fields):
                row = (which * fields + f) * fields + g
                table[row : row + 1, :] = jnp.full((1, LANES), matrix[f, g], jnp.float32)
    rows = block_rows(fields, cells)
    if width < LANES or rows > fields * (CELL_KINDS * cells + cells + 1):
        blocks[...] = jnp.zeros_like(blocks)
    pad[...] = jnp.zeros_like(pad)
    for f in range(fields):
        pad[f, 1 : cells + 1, :] = adj[f]
    ahead = [pad[f, 2 : cells + 2, :] for f in range(fields)]
    behind = [pad[f, 0:cells, :] for f in range(fields)]
    central = mix(scalars(jac), [a - b for a, b in zip(ahead, behind)])
    residual = [
        src[f] - 0.5 * central[f] + dissipation * (ahead[f] - 2.0 * adj[f] + behind[f])
        for f in range(fields)
    ]
    characteristic = mix(scalars(left), residual)
    cell = lax.broadcasted_iota(jnp.int32, (cells, length), 0)
    extra = CELL_KINDS * fields * cells
    for f in range(fields):
        diagonal = up[0, f]
        inverse = 1.0 / diagonal
        own = jnp.where(cell == 1, inverse, 1.0)
        diagonal_1 = jnp.broadcast_to(up[0, f, 1:2, :], (cells, length))
        values = (
            characteristic[f] * own,
            low[0, f] * jnp.where(cell == 2, diagonal_1, own),
            low[1, f] * jnp.where(cell == 3, diagonal_1, own),
            up[1, f] * inverse,
            up[2, f] * inverse,
        )
        for d, base, lanes, to in pieces(group, width, rows):
            for k, value in enumerate(values):
                at = base + (k * fields + f) * cells
                blocks[d, at : at + cells, to] = value[:, lanes]
            at = base + extra + f * (cells + 1)
            blocks[d, at : at + 1, to] = inverse[0:1, lanes]
            blocks[d, at + 1 : at + cells - 1, to] = inverse[2:cells, lanes]
            blocks[d, at + cells - 1 : at + cells, to] = adj[f, 0:1, lanes]
            blocks[d, at + cells : at + cells + 1, to] = adj[f, cells - 1 : cells, lanes]
    spread(blocks, me, outs)


def pieces(group, width, rows):
    step = min(width, LANES)
    for d in range(group):
        for b in range(width // step):
            start = d * width + b * step
            yield d, b * rows, slice(start, start + step), slice(0, step)


class Lines:
    def __init__(self, ref, fields, cells, base):
        self.ref, self.fields, self.cells, self.base = ref, fields, cells, base

    def value(self, d, k, i):
        at = self.base(d) + k * self.fields * self.cells + i
        return self.ref[pl.ds(at, self.fields, stride=self.cells), :]

    def divided(self, d, i, value):
        if i == 1:
            return value
        at = self.base(d) + CELL_KINDS * self.fields * self.cells + (i if i == 0 else i - 1)
        return value * self.ref[pl.ds(at, self.fields, stride=self.cells + 1), :]


def less(value, factor, other):
    if other is None:
        return value
    return -(factor * other) if value is None else value - factor * other


SLOTS = 8


def sweep_kernel(group, fields, cells, me, half, table, *refs):
    jac, left = table_entries(table, fields, 0), table_entries(table, fields, 1)
    received, (lines, edge, message) = refs[:group], refs[group:]
    rows = block_rows(fields, cells)
    size = received[0].shape[0]
    count = size // rows
    for k in range(group):
        at = pl.multiple_of(lax.bitwise_xor(me[0], k) * size, SUBLANES)
        lines[pl.ds(at, size), :] = received[k][...]
    lower_half = jnp.full((fields, LANES), half[0], jnp.int32) == 0
    extra = CELL_KINDS * fields * cells
    for b in range(count):

        def across(row):
            return lines[pl.ds(b * rows + row, group, stride=size), :]

        firsts = [across(extra + f * (cells + 1) + cells - 1) for f in range(fields)]
        lasts = [across(extra + f * (cells + 1) + cells) for f in range(fields)]
        from_last = mix(jac, lasts)
        from_first = mix(jac, firsts)
        into_first = mix(left, [0.5 * x + dissipation * y for x, y in zip(from_last, lasts)])
        into_last = mix(left, [dissipation * y - 0.5 * x for x, y in zip(from_first, firsts)])
        at = 2 * b * fields * group
        for f in range(fields):
            edge[at + f * group : at + (f + 1) * group, :] = into_first[f]
            edge[at + (fields + f) * group : at + (fields + f + 1) * group, :] = into_last[f]

        def to_next(d):
            return edge[pl.ds(at + d, fields, stride=group), :]

        def to_previous(d):
            return edge[pl.ds(at + fields * group + d, fields, stride=group), :]

        view = Lines(lines, fields, cells, lambda d: (d * count + b) * rows)
        ones = jnp.ones((fields, LANES), jnp.float32)
        one, two = [None, ones, None], [None, None, None]
        forward = {}
        for d in range(group):
            for i in range(cells):
                value = view.value(d, 0, i)
                if i == 0 and d > 0:
                    value = value + to_next(d - 1)
                if i == cells - 1 and d < group - 1:
                    value = value + to_previous(d + 1)
                start = [value, None, ones if d == 0 and i == 0 else None]
                first, second = view.value(d, 1, i), view.value(d, 2, i)
                now = [less(less(start[c], second, two[c]), first, one[c]) for c in range(3)]
                forward[d, i] = now
                one, two = now, one
        ends = [one[0], two[0], to_next(group - 1)]
        one, two = [None] * 3, [None] * 3
        for d in reversed(range(group)):
            for i in reversed(range(cells)):
                start = [view.divided(d, i, value) for value in forward[d, i]]
                first, second = view.value(d, 3, i), view.value(d, 4, i)
                now = [less(less(start[c], second, two[c]), first, one[c]) for c in range(3)]
                one, two = now, one
        begins = [one[0], two[0], to_previous(0)]
        slots = [jnp.where(lower_half, x, y) for x, y in zip(ends, begins)]
        slots += [one[1], two[1], one[2], two[2], view.value(0, 2, 0)]
        for k, value in enumerate(slots):
            row = (b * SLOTS + k) * fields
            message[row : row + fields, :] = value


def solve_kernel(group, fields, cells, me, half, table, lines, edge, mine, other, *refs):
    outs, (squares, whole, blocks) = refs[:group], refs[group:]
    rows = block_rows(fields, cells)
    size = lines.shape[0] // group
    count = size // rows
    total = group * cells
    lower_half = jnp.full((fields, LANES), half[0], jnp.int32) == 0
    summed = None
    for b in range(count):
        view = Lines(lines, fields, cells, lambda d: (d * count + b) * rows)
        at = 2 * b * fields * group

        def to_next(d):
            return edge[pl.ds(at + d, fields, stride=group), :]

        def to_previous(d):
            return edge[pl.ds(at + fields * group + d, fields, stride=group), :]

        def slot(ref, k):
            row = (b * SLOTS + k) * fields
            return ref[row : row + fields, :]

        def of_lower(k):
            return jnp.where(lower_half, slot(mine, k), slot(other, k))

        def of_upper(k):
            return jnp.where(lower_half, slot(other, k), slot(mine, k))

        zeros = jnp.zeros((fields, LANES), jnp.float32)
        onto_last, onto_first = of_upper(2), of_lower(2)
        before, before_2 = of_lower(0) + onto_last, of_lower(1)
        added = onto_first - of_upper(7) * before_2
        after = of_upper(0) + of_upper(3) * before + of_upper(5) * added
        after_2 = of_upper(1) + of_upper(4) * before + of_upper(6) * added
        one, two = jnp.where(lower_half, zeros, before), jnp.where(lower_half, zeros, before_2)
        onto_first = jnp.where(lower_half, zeros, onto_first)
        onto_last = jnp.where(lower_half, onto_last, zeros)
        forward = {}
        for d in range(group):
            for i in range(cells):
                value = view.value(d, 0, i)
                if i == 0:
                    value = value + (to_next(d - 1) if d > 0 else onto_first)
                if i == cells - 1:
                    value = value + (to_previous(d + 1) if d < group - 1 else onto_last)
                value = less(less(value, view.value(d, 2, i), two), view.value(d, 1, i), one)
                forward[d, i] = value
                one, two = value, one
        one, two = jnp.where(lower_half, after, zeros), jnp.where(lower_half, after_2, zeros)
        for d in reversed(range(group)):
            for i in reversed(range(cells)):
                value = view.divided(d, i, forward[d, i])
                value = less(less(value, view.value(d, 4, i), two), view.value(d, 3, i), one)
                whole[pl.ds(b * fields * total + d * cells + i, fields, stride=total), :] = value
                one, two = value, one
        columns = [(b * fields + g) * total for g in range(fields)]
        increment = mix(table_entries(table, fields, 2), [whole[at : at + total, :] for at in columns])
        for f in range(fields):
            part = jnp.sum(increment[f] * increment[f], axis=0, keepdims=True)
            summed = part if summed is None else summed + part
            for d in range(group):
                row = (b * fields + f) * cells
                blocks[d, row : row + cells, :] = increment[f][d * cells : (d + 1) * cells, :]
    spread(blocks, me, outs)
    for n in range(squares.shape[0]):
        squares[n] = summed


def slab_kernel(peers, me, adj, grad, ctrl, *outs):
    fields, cells, length = adj.shape
    height = outs[0].shape[0]
    contribution = adj[0] * grad[0]
    for f in range(1, fields):
        contribution = contribution + adj[f] * grad[f]
    upper = contribution.astype(jnp.bfloat16).astype(jnp.float32)
    lower = contribution - upper
    high = lax.shift_right_logical(ctrl[...], 7)
    low = lax.bitwise_and(ctrl[...], LANES - 1)
    block = lax.broadcasted_iota(jnp.int32, (height, length), 0)
    lane = lax.broadcasted_iota(jnp.int32, (LANES, length), 0)
    sums = None
    for i in range(cells):
        hit = lane == low[i : i + 1, :]
        terms = jnp.concatenate(
            [
                jnp.where(hit, upper[i : i + 1, :], 0.0).astype(jnp.bfloat16),
                jnp.where(hit, lower[i : i + 1, :], 0.0).astype(jnp.bfloat16),
            ],
            axis=0,
        )
        rows = []
        for k in range(peers):
            offset = lax.bitwise_xor(me[0], k) * height
            rows.append(jnp.where(block == high[i : i + 1, :] - offset, 1.0, 0.0).astype(jnp.bfloat16))
        picked = jnp.concatenate(rows, axis=0)
        part = lax.dot_general(
            picked, terms, (((1,), (1,)), ((), ())), preferred_element_type=jnp.float32
        )
        sums = part if sums is None else sums + part
    sums = sums[:, :LANES] + sums[:, LANES:]
    for k in range(peers):
        outs[k][...] = sums[k * height : (k + 1) * height, :]


def finish_kernel(group, width, peers, cell_count, me, adj, squares, *refs):
    moved, slabs, (out, sens, blocks) = refs[:group], refs[group : group + peers], refs[group + peers :]
    fields, cells, _ = adj.shape
    for k in range(group):
        blocks[lax.bitwise_xor(me[0], k)] = moved[k][...]
    slab = slabs[0][...]
    for k in range(1, peers):
        slab = slab + slabs[k][...]
    sens[...] = slab
    total = jnp.sum(jnp.sum(squares[...], axis=0), axis=1, keepdims=True)
    factor = step_scale / jnp.sqrt(total / cell_count + epsilon)
    for d, base, lanes, to in pieces(group, width, fields * cells):
        for f in range(fields):
            at = base + f * cells
            out[f, :, lanes] = adj[f, :, lanes] + factor * blocks[d, at : at + cells, to]


def swap(array, axis, k):
    return lax.ppermute(array, axis, [(i, i ^ k) for i in range(lax.axis_size(axis))])


def exchange(arrays, axis):
    out = [arrays[0]]
    for k in range(1, len(arrays)):
        out.append(swap(arrays[k], axis, k))
    return out


def step(
    adjoint, source, shape_grad, lower_band, upper_band, jacobian, left_vectors, right_vectors, ctrl_local
):
    fields, cells, length = adjoint.shape
    parts, peers = lax.axis_size("stream"), lax.axis_size("cross")
    group = parts // 2
    width = length // group
    count = -(-width // LANES)
    rows = count * block_rows(fields, cells)
    back = count * fields * cells
    f32 = jnp.float32

    at = lax.axis_index("stream").astype(jnp.int32)
    me, half = lax.rem(at, group).reshape(1), lax.div(at, group).reshape(1)
    *packed, table = pl.pallas_call(
        functools.partial(pack_kernel, group, width),
        out_shape=[pltpu.VMEM((rows, LANES), f32)] * group
        + [pltpu.VMEM((table_rows(fields), LANES), f32)],
        in_specs=[SMEM] * 4 + [VMEM] * 4,
        out_specs=[VMEM] * (group + 1),
        scratch_shapes=[
            pltpu.VMEM((group, rows, LANES), f32),
            pltpu.VMEM((fields, round_up(cells + 2, SUBLANES), length), f32),
        ],
        name="pack",
    )(me, jacobian, left_vectors, right_vectors, adjoint, source, lower_band, upper_band)
    received = exchange(packed, "stream")

    height = NCTRL // (parts * peers * LANES)
    column = lax.axis_index("cross").astype(jnp.int32).reshape(1)
    slabs = pl.pallas_call(
        functools.partial(slab_kernel, peers),
        out_shape=[pltpu.VMEM((height, LANES), f32)] * peers,
        in_specs=[SMEM, VMEM, VMEM, VMEM],
        out_specs=[VMEM] * peers,
        cost_estimate=pl.CostEstimate(
            flops=4 * cells * length * NCTRL // parts, bytes_accessed=4 << 20, transcendentals=0
        ),
        name="slab",
    )(column, held(adjoint), shape_grad, ctrl_local)

    lines, edge, message = pl.pallas_call(
        functools.partial(sweep_kernel, group, fields, cells),
        out_shape=[
            pltpu.VMEM((group * rows, LANES), f32),
            pltpu.VMEM((2 * count * fields * group, LANES), f32),
            pltpu.VMEM((count * SLOTS * fields, LANES), f32),
        ],
        in_specs=[SMEM] * 2 + [VMEM] * (1 + group),
        out_specs=[VMEM] * 3,
        name="sweep",
    )(me, half, *(held(a) for a in (table, *received)))
    other = swap(message, "stream", group)
    slabs = exchange(slabs, "cross")

    *moved, squares = pl.pallas_call(
        functools.partial(solve_kernel, group, fields, cells),
        out_shape=[pltpu.VMEM((back, LANES), f32)] * group
        + [pltpu.VMEM((parts * peers, 1, LANES), f32)],
        in_specs=[SMEM] * 2 + [VMEM] * 5,
        out_specs=[VMEM] * (group + 1),
        scratch_shapes=[
            pltpu.VMEM((count * fields * group * cells, LANES), f32),
            pltpu.VMEM((group, back, LANES), f32),
        ],
        name="solve",
    )(me, half, *(held(a) for a in (table, lines, edge, message, other)))
    squares = lax.all_to_all(squares, ("stream", "cross"), split_axis=0, concat_axis=0, tiled=True)
    moved = exchange(moved, "stream")

    cell_count = fields * cells * length * parts * peers
    adjoint_next, sensitivity = pl.pallas_call(
        functools.partial(finish_kernel, group, width, peers, cell_count),
        out_shape=[
            jax.ShapeDtypeStruct(adjoint.shape, f32),
            jax.ShapeDtypeStruct((height, LANES), f32),
        ],
        in_specs=[SMEM] + [VMEM] * (2 + group + peers),
        out_specs=[VMEM, VMEM],
        scratch_shapes=[pltpu.VMEM((group, back, LANES), f32)],
        name="finish",
    )(me, *(held(a) for a in (adjoint, squares, *moved, *slabs)))
    return adjoint_next, sensitivity.reshape(height * LANES)


def solution(mesh):
    in_specs = (
        P(None, "stream", "cross"),
        P(None, "stream", "cross"),
        P(None, "stream", "cross"),
        P(None, None, "stream", "cross"),
        P(None, None, "stream", "cross"),
        P(),
        P(),
        P(),
        P("stream", "cross"),
    )
    out_specs = (P(None, "stream", "cross"), P(("stream", "cross")))
    return jax.shard_map(step, mesh=mesh, in_specs=in_specs, out_specs=out_specs, check_vma=False)
```

```python
import functools

import jax
import jax.numpy as jnp
from jax import lax
from jax.experimental import pallas as pl
from jax.experimental.pallas import tpu as pltpu
from jax.sharding import PartitionSpec as P


NCTRL = 524288
LANES = 128
SUBLANES = 8

dissipation = 0.25
step_scale = 0.5
epsilon = 1e-06


VMEM = pl.BlockSpec(memory_space=pltpu.VMEM)
SMEM = pl.BlockSpec(memory_space=pltpu.SMEM)
ANY = pl.BlockSpec(memory_space=pl.ANY)


def held(array):
    return pltpu.with_memory_space_constraint(array, pltpu.VMEM)


def round_up(value, step):
    return -(-value // step) * step


def mix(entry, columns):
    count = len(columns)
    return [
        sum(entry(f, g) * columns[g] for g in range(1, count)) + entry(f, 0) * columns[0]
        for f in range(count)
    ]


def scalars(matrix):
    return lambda f, g: matrix[f, g]


def table_rows(fields):
    return round_up(3 * fields * fields, SUBLANES)


def table_entries(table, fields, which):
    def entry(f, g):
        row = (which * fields + f) * fields + g
        return table[row : row + 1, :]

    return entry


CELL_KINDS = 5


def block_rows(fields, cells):
    return round_up(fields * (CELL_KINDS * cells + cells - 1 + 2), SUBLANES)


def spread(scratch, me, outs):
    for k, out in enumerate(outs):
        out[...] = scratch[lax.bitwise_xor(me[0], k)]


def pack_kernel(group, width, me, *refs):
    sources, outs = refs[:7], refs[7 : 7 + group]
    table, blocks, pad, jac, left, right, adj, src, low, up, arrived = refs[7 + group :]
    copies = [
        pltpu.make_async_copy(source, target, arrived.at[n])
        for n, (source, target) in enumerate(zip(sources, (jac, left, right, adj, src, low, up)))
    ]
    for n in (3, 4, 0, 1, 2, 6, 5):
        copies[n].start()
    fields, cells, length = adj.shape
    rows = block_rows(fields, cells)
    if width < LANES or rows > fields * (CELL_KINDS * cells + cells + 1):
        blocks[...] = jnp.zeros_like(blocks)
    pad[...] = jnp.zeros_like(pad)
    cell = lax.broadcasted_iota(jnp.int32, (cells, length), 0)
    extra = CELL_KINDS * fields * cells
    copies[3].wait()
    for f in range(fields):
        pad[f, 1 : cells + 1, :] = adj[f]
        for d, base, lanes, to in pieces(group, width, rows):
            at = base + extra + f * (cells + 1) + cells - 1
            blocks[d, at : at + 1, to] = adj[f, 0:1, lanes]
            blocks[d, at + 1 : at + 2, to] = adj[f, cells - 1 : cells, lanes]
    for n in (4, 0, 1, 2):
        copies[n].wait()
    for which, matrix in enumerate((jac, left, right)):
        for f in range(fields):
            for g in range(fields):
                row = (which * fields + f) * fields + g
                table[row : row + 1, :] = jnp.full((1, LANES), matrix[f, g], jnp.float32)
    ahead = [pad[f, 2 : cells + 2, :] for f in range(fields)]
    behind = [pad[f, 0:cells, :] for f in range(fields)]
    central = mix(scalars(jac), [a - b for a, b in zip(ahead, behind)])
    residual = [
        src[f] - 0.5 * central[f] + dissipation * (ahead[f] - 2.0 * adj[f] + behind[f])
        for f in range(fields)
    ]
    characteristic = mix(scalars(left), residual)
    copies[6].wait()
    copies[5].wait()
    for f in range(fields):
        diagonal = up[0, f]
        inverse = 1.0 / diagonal
        own = jnp.where(cell == 1, inverse, 1.0)
        diagonal_1 = jnp.broadcast_to(up[0, f, 1:2, :], (cells, length))
        values = (
            characteristic[f] * own,
            low[0, f] * jnp.where(cell == 2, diagonal_1, own),
            low[1, f] * jnp.where(cell == 3, diagonal_1, own),
            up[1, f] * inverse,
            up[2, f] * inverse,
        )
        for d, base, lanes, to in pieces(group, width, rows):
            for k, value in enumerate(values):
                at = base + (k * fields + f) * cells
                blocks[d, at : at + cells, to] = value[:, lanes]
            at = base + extra + f * (cells + 1)
            blocks[d, at : at + 1, to] = inverse[0:1, lanes]
            blocks[d, at + 1 : at + cells - 1, to] = inverse[2:cells, lanes]
    spread(blocks, me, outs)


def pieces(group, width, rows):
    step = min(width, LANES)
    for d in range(group):
        for b in range(width // step):
            start = d * width + b * step
            yield d, b * rows, slice(start, start + step), slice(0, step)


class Lines:
    def __init__(self, ref, fields, cells, base):
        self.ref, self.fields, self.cells, self.base = ref, fields, cells, base

    def value(self, d, k, i):
        at = self.base(d) + k * self.fields * self.cells + i
        return self.ref[pl.ds(at, self.fields, stride=self.cells), :]

    def divided(self, d, i, value):
        if i == 1:
            return value
        at = self.base(d) + CELL_KINDS * self.fields * self.cells + (i if i == 0 else i - 1)
        return value * self.ref[pl.ds(at, self.fields, stride=self.cells + 1), :]


def less(value, factor, other):
    if other is None:
        return value
    return -(factor * other) if value is None else value - factor * other


SLOTS = 8


def sweep_kernel(group, fields, cells, me, half, table, *refs):
    jac, left = table_entries(table, fields, 0), table_entries(table, fields, 1)
    received, (lines, edge, message) = refs[:group], refs[group:]
    rows = block_rows(fields, cells)
    size = received[0].shape[0]
    count = size // rows
    for k in range(group):
        at = pl.multiple_of(lax.bitwise_xor(me[0], k) * size, SUBLANES)
        lines[pl.ds(at, size), :] = received[k][...]
    lower_half = jnp.full((fields, LANES), half[0], jnp.int32) == 0
    extra = CELL_KINDS * fields * cells
    for b in range(count):

        def across(row):
            return lines[pl.ds(b * rows + row, group, stride=size), :]

        firsts = [across(extra + f * (cells + 1) + cells - 1) for f in range(fields)]
        lasts = [across(extra + f * (cells + 1) + cells) for f in range(fields)]
        from_last = mix(jac, lasts)
        from_first = mix(jac, firsts)
        into_first = mix(left, [0.5 * x + dissipation * y for x, y in zip(from_last, lasts)])
        into_last = mix(left, [dissipation * y - 0.5 * x for x, y in zip(from_first, firsts)])
        at = 2 * b * fields * group
        for f in range(fields):
            edge[at + f * group : at + (f + 1) * group, :] = into_first[f]
            edge[at + (fields + f) * group : at + (fields + f + 1) * group, :] = into_last[f]

        def to_next(d):
            return edge[pl.ds(at + d, fields, stride=group), :]

        def to_previous(d):
            return edge[pl.ds(at + fields * group + d, fields, stride=group), :]

        view = Lines(lines, fields, cells, lambda d: (d * count + b) * rows)
        ones = jnp.ones((fields, LANES), jnp.float32)
        one, two = [None, ones, None], [None, None, None]
        forward = {}
        for d in range(group):
            for i in range(cells):
                value = view.value(d, 0, i)
                if i == 0 and d > 0:
                    value = value + to_next(d - 1)
                if i == cells - 1 and d < group - 1:
                    value = value + to_previous(d + 1)
                start = [value, None, ones if d == 0 and i == 0 else None]
                first, second = view.value(d, 1, i), view.value(d, 2, i)
                now = [less(less(start[c], second, two[c]), first, one[c]) for c in range(3)]
                forward[d, i] = now
                one, two = now, one
        ends = [one[0], two[0], to_next(group - 1)]
        one, two = [None] * 3, [None] * 3
        for d in reversed(range(group)):
            for i in reversed(range(cells)):
                start = [view.divided(d, i, value) for value in forward[d, i]]
                first, second = view.value(d, 3, i), view.value(d, 4, i)
                now = [less(less(start[c], second, two[c]), first, one[c]) for c in range(3)]
                one, two = now, one
        begins = [one[0], two[0], to_previous(0)]
        slots = [jnp.where(lower_half, x, y) for x, y in zip(ends, begins)]
        slots += [one[1], two[1], one[2], two[2], view.value(0, 2, 0)]
        for k, value in enumerate(slots):
            row = (b * SLOTS + k) * fields
            message[row : row + fields, :] = value


def solve_kernel(group, fields, cells, me, half, table, lines, edge, mine, other, *refs):
    outs, (squares, whole, blocks) = refs[:group], refs[group:]
    rows = block_rows(fields, cells)
    size = lines.shape[0] // group
    count = size // rows
    total = group * cells
    lower_half = jnp.full((fields, LANES), half[0], jnp.int32) == 0
    summed = None
    for b in range(count):
        view = Lines(lines, fields, cells, lambda d: (d * count + b) * rows)
        at = 2 * b * fields * group

        def to_next(d):
            return edge[pl.ds(at + d, fields, stride=group), :]

        def to_previous(d):
            return edge[pl.ds(at + fields * group + d, fields, stride=group), :]

        def slot(ref, k):
            row = (b * SLOTS + k) * fields
            return ref[row : row + fields, :]

        def of_lower(k):
            return jnp.where(lower_half, slot(mine, k), slot(other, k))

        def of_upper(k):
            return jnp.where(lower_half, slot(other, k), slot(mine, k))

        zeros = jnp.zeros((fields, LANES), jnp.float32)
        onto_last, onto_first = of_upper(2), of_lower(2)
        before, before_2 = of_lower(0) + onto_last, of_lower(1)
        added = onto_first - of_upper(7) * before_2
        after = of_upper(0) + of_upper(3) * before + of_upper(5) * added
        after_2 = of_upper(1) + of_upper(4) * before + of_upper(6) * added
        one, two = jnp.where(lower_half, zeros, before), jnp.where(lower_half, zeros, before_2)
        onto_first = jnp.where(lower_half, zeros, onto_first)
        onto_last = jnp.where(lower_half, onto_last, zeros)
        forward = {}
        for d in range(group):
            for i in range(cells):
                value = view.value(d, 0, i)
                if i == 0:
                    value = value + (to_next(d - 1) if d > 0 else onto_first)
                if i == cells - 1:
                    value = value + (to_previous(d + 1) if d < group - 1 else onto_last)
                value = less(less(value, view.value(d, 2, i), two), view.value(d, 1, i), one)
                forward[d, i] = value
                one, two = value, one
        one, two = jnp.where(lower_half, after, zeros), jnp.where(lower_half, after_2, zeros)
        for d in reversed(range(group)):
            for i in reversed(range(cells)):
                value = view.divided(d, i, forward[d, i])
                value = less(less(value, view.value(d, 4, i), two), view.value(d, 3, i), one)
                whole[pl.ds(b * fields * total + d * cells + i, fields, stride=total), :] = value
                one, two = value, one
        columns = [(b * fields + g) * total for g in range(fields)]
        increment = mix(table_entries(table, fields, 2), [whole[at : at + total, :] for at in columns])
        for f in range(fields):
            part = jnp.sum(increment[f] * increment[f], axis=0, keepdims=True)
            summed = part if summed is None else summed + part
            for d in range(group):
                row = (b * fields + f) * cells
                blocks[d, row : row + cells, :] = increment[f][d * cells : (d + 1) * cells, :]
    spread(blocks, me, outs)
    for n in range(squares.shape[0]):
        squares[n] = summed


def slab_kernel(peers, me, adj, grad, ctrl, keep, send):
    fields, cells, length = adj.shape
    height = keep.shape[0] * 2 // peers
    contribution = adj[0] * grad[0]
    for f in range(1, fields):
        contribution = contribution + adj[f] * grad[f]
    upper = contribution.astype(jnp.bfloat16).astype(jnp.float32)
    lower = contribution - upper
    high = lax.shift_right_logical(ctrl[...], 7)
    low = lax.bitwise_and(ctrl[...], LANES - 1)
    block = lax.broadcasted_iota(jnp.int32, (height, length), 0)
    lane = lax.broadcasted_iota(jnp.int32, (LANES, length), 0)
    sums = None
    for i in range(cells):
        hit = lane == low[i : i + 1, :]
        terms = jnp.concatenate(
            [
                jnp.where(hit, upper[i : i + 1, :], 0.0).astype(jnp.bfloat16),
                jnp.where(hit, lower[i : i + 1, :], 0.0).astype(jnp.bfloat16),
            ],
            axis=0,
        )
        rows = []
        for k in range(peers):
            offset = lax.bitwise_xor(me[0], k) * height
            rows.append(jnp.where(block == high[i : i + 1, :] - offset, 1.0, 0.0).astype(jnp.bfloat16))
        picked = jnp.concatenate(rows, axis=0)
        part = lax.dot_general(
            picked, terms, (((1,), (1,)), ((), ())), preferred_element_type=jnp.float32
        )
        sums = part if sums is None else sums + part
    sums = sums[:, :LANES] + sums[:, LANES:]
    for k in range(peers):
        out, at = (send if k % 2 else keep), k // 2 * height
        out[at : at + height, :] = sums[k * height : (k + 1) * height, :]


def halve_kernel(height, kept, received, keep, send):
    for k in range(kept.shape[0] // height):
        rows = slice(k * height, (k + 1) * height)
        out, at = (send if k % 2 else keep), k // 2 * height
        out[at : at + height, :] = kept[rows, :] + received[rows, :]


def finish_kernel(group, width, cell_count, me, adj, squares, keep, gained, *refs):
    moved, (out, sens, blocks) = refs[:group], refs[group:]
    fields, cells, _ = adj.shape
    for k in range(group):
        blocks[lax.bitwise_xor(me[0], k)] = moved[k][...]
    sens[...] = keep[...] + gained[...]
    total = jnp.sum(jnp.sum(squares[...], axis=0), axis=1, keepdims=True)
    factor = step_scale / jnp.sqrt(total / cell_count + epsilon)
    for d, base, lanes, to in pieces(group, width, fields * cells):
        for f in range(fields):
            at = base + f * cells
            out[f, :, lanes] = adj[f, :, lanes] + factor * blocks[d, at : at + cells, to]


def swap(array, axis, k):
    return lax.ppermute(array, axis, [(i, i ^ k) for i in range(lax.axis_size(axis))])


def exchange(arrays, axis):
    out = [arrays[0]]
    for k in range(1, len(arrays)):
        out.append(swap(arrays[k], axis, k))
    return out


def step(
    adjoint, source, shape_grad, lower_band, upper_band, jacobian, left_vectors, right_vectors, ctrl_local
):
    fields, cells, length = adjoint.shape
    parts, peers = lax.axis_size("stream"), lax.axis_size("cross")
    group = parts // 2
    width = length // group
    count = -(-width // LANES)
    rows = count * block_rows(fields, cells)
    back = count * fields * cells
    f32 = jnp.float32

    at = lax.axis_index("stream").astype(jnp.int32)
    me = lax.rem(at, group).reshape(1)
    half = lax.div(at, group)
    half = half.reshape(1)
    *packed, table = pl.pallas_call(
        functools.partial(pack_kernel, group, width),
        out_shape=[pltpu.VMEM((rows, LANES), f32)] * group
        + [pltpu.VMEM((table_rows(fields), LANES), f32)],
        in_specs=[SMEM] + [ANY] * 7,
        out_specs=[VMEM] * (group + 1),
        scratch_shapes=[
            pltpu.VMEM((group, rows, LANES), f32),
            pltpu.VMEM((fields, round_up(cells + 2, SUBLANES), length), f32),
        ]
        + [pltpu.SMEM((fields, fields), f32)] * 3
        + [
            pltpu.VMEM(array.shape, f32) for array in (adjoint, source, lower_band, upper_band)
        ]
        + [pltpu.SemaphoreType.DMA((7,))],
        name="pack",
    )(me, jacobian, left_vectors, right_vectors, adjoint, source, lower_band, upper_band)
    received = exchange(packed, "stream")

    height = NCTRL // (parts * peers * LANES)
    column = lax.axis_index("cross").astype(jnp.int32).reshape(1)
    keep, send = pl.pallas_call(
        functools.partial(slab_kernel, peers),
        out_shape=[pltpu.VMEM((peers // 2 * height, LANES), f32)] * 2,
        in_specs=[SMEM, VMEM, VMEM, VMEM],
        out_specs=[VMEM] * 2,
        cost_estimate=pl.CostEstimate(
            flops=4 * cells * length * NCTRL // parts, bytes_accessed=4 << 20, transcendentals=0
        ),
        name="slab",
    )(column, held(adjoint), shape_grad, ctrl_local)

    bit = 1
    while True:
        gained = swap(send, "cross", bit)
        bit *= 2
        if bit == peers:
            break
        keep, send = pl.pallas_call(
            functools.partial(halve_kernel, height),
            out_shape=[pltpu.VMEM((peers // bit // 2 * height, LANES), f32)] * 2,
            in_specs=[VMEM] * 2,
            out_specs=[VMEM] * 2,
        )(held(keep), held(gained))

    lines, edge, message = pl.pallas_call(
        functools.partial(sweep_kernel, group, fields, cells),
        out_shape=[
            pltpu.VMEM((group * rows, LANES), f32),
            pltpu.VMEM((2 * count * fields * group, LANES), f32),
            pltpu.VMEM((count * SLOTS * fields, LANES), f32),
        ],
        in_specs=[SMEM] * 2 + [VMEM] * (1 + group),
        out_specs=[VMEM] * 3,
        name="sweep",
    )(me, half, *(held(a) for a in (table, *received)))
    other = swap(message, "stream", group)

    *moved, squares = pl.pallas_call(
        functools.partial(solve_kernel, group, fields, cells),
        out_shape=[pltpu.VMEM((back, LANES), f32)] * group
        + [pltpu.VMEM((parts * peers, 1, LANES), f32)],
        in_specs=[SMEM] * 2 + [VMEM] * 5,
        out_specs=[VMEM] * (group + 1),
        scratch_shapes=[
            pltpu.VMEM((count * fields * group * cells, LANES), f32),
            pltpu.VMEM((group, back, LANES), f32),
        ],
        name="solve",
    )(me, half, *(held(a) for a in (table, lines, edge, message, other)))
    squares = lax.all_to_all(squares, ("stream", "cross"), split_axis=0, concat_axis=0, tiled=True)
    moved = exchange(moved, "stream")

    cell_count = fields * cells * length * parts * peers
    adjoint_next, sensitivity = pl.pallas_call(
        functools.partial(finish_kernel, group, width, cell_count),
        out_shape=[
            jax.ShapeDtypeStruct(adjoint.shape, f32),
            jax.ShapeDtypeStruct((height, LANES), f32),
        ],
        in_specs=[SMEM] + [VMEM] * (4 + group),
        out_specs=[VMEM, VMEM],
        scratch_shapes=[pltpu.VMEM((group, back, LANES), f32)],
        name="finish",
    )(me, *(held(a) for a in (adjoint, squares, keep, gained, *moved)))
    return adjoint_next, sensitivity.reshape(height * LANES)


def solution(mesh):
    in_specs = (
        P(None, "stream", "cross"),
        P(None, "stream", "cross"),
        P(None, "stream", "cross"),
        P(None, None, "stream", "cross"),
        P(None, None, "stream", "cross"),
        P(),
        P(),
        P(),
        P("stream", "cross"),
    )
    out_specs = (P(None, "stream", "cross"), P(("stream", "cross")))
    return jax.shard_map(step, mesh=mesh, in_specs=in_specs, out_specs=out_specs, check_vma=False)
```

```python
import functools

import jax
import jax.numpy as jnp
from jax import lax
from jax.experimental import pallas as pl
from jax.experimental.pallas import tpu as pltpu
from jax.sharding import PartitionSpec as P


NCTRL = 524288
LANES = 128
SUBLANES = 8

dissipation = 0.25
step_scale = 0.5
epsilon = 1e-06


VMEM = pl.BlockSpec(memory_space=pltpu.VMEM)
SMEM = pl.BlockSpec(memory_space=pltpu.SMEM)


def held(array):
    return pltpu.with_memory_space_constraint(array, pltpu.VMEM)


def round_up(value, step):
    return -(-value // step) * step


def mix(entry, columns):
    count = len(columns)
    return [
        sum(entry(f, g) * columns[g] for g in range(1, count)) + entry(f, 0) * columns[0]
        for f in range(count)
    ]


def scalars(matrix):
    return lambda f, g: matrix[f, g]


def table_rows(fields):
    return round_up(3 * fields * fields, SUBLANES)


def table_entries(table, fields, which):
    def entry(f, g):
        row = (which * fields + f) * fields + g
        return table[row : row + 1, :]

    return entry


CELL_KINDS = 5


def block_rows(fields, cells):
    return round_up(fields * (CELL_KINDS * cells + cells - 1 + 2), SUBLANES)


def spread(scratch, me, outs):
    for k, out in enumerate(outs):
        out[...] = scratch[lax.bitwise_xor(me[0], k)]


def pack_kernel(group, width, me, jac, left, right, adj, src, low, up, *refs):
    outs, (table, blocks, pad) = refs[:group], refs[group:]
    fields, cells, length = adj.shape
    for which, matrix in enumerate((jac, left, right)):
        for f in range(fields):
            for g in range(fields):
                row = (which * fields + f) * fields + g
                table[row : row + 1, :] = jnp.full((1, LANES), matrix[f, g], jnp.float32)
    rows = block_rows(fields, cells)
    if width < LANES or rows > fields * (CELL_KINDS * cells + cells + 1):
        blocks[...] = jnp.zeros_like(blocks)
    pad[...] = jnp.zeros_like(pad)
    for f in range(fields):
        pad[f, 1 : cells + 1, :] = adj[f]
    ahead = [pad[f, 2 : cells + 2, :] for f in range(fields)]
    behind = [pad[f, 0:cells, :] for f in range(fields)]
    central = mix(scalars(jac), [a - b for a, b in zip(ahead, behind)])
    residual = [
        src[f] - 0.5 * central[f] + dissipation * (ahead[f] - 2.0 * adj[f] + behind[f])
        for f in range(fields)
    ]
    characteristic = mix(scalars(left), residual)
    cell = lax.broadcasted_iota(jnp.int32, (cells, length), 0)
    extra = CELL_KINDS * fields * cells
    for f in range(fields):
        diagonal = up[0, f]
        inverse = 1.0 / diagonal
        own = jnp.where(cell == 1, inverse, 1.0)
        diagonal_1 = jnp.broadcast_to(up[0, f, 1:2, :], (cells, length))
        values = (
            characteristic[f] * own,
            low[0, f] * jnp.where(cell == 2, diagonal_1, own),
            low[1, f] * jnp.where(cell == 3, diagonal_1, own),
            up[1, f] * inverse,
            up[2, f] * inverse,
        )
        for d, base, lanes, to in pieces(group, width, rows):
            for k, value in enumerate(values):
                at = base + (k * fields + f) * cells
                blocks[d, at : at + cells, to] = value[:, lanes]
            at = base + extra + f * (cells + 1)
            blocks[d, at : at + 1, to] = inverse[0:1, lanes]
            blocks[d, at + 1 : at + cells - 1, to] = inverse[2:cells, lanes]
            blocks[d, at + cells - 1 : at + cells, to] = adj[f, 0:1, lanes]
            blocks[d, at + cells : at + cells + 1, to] = adj[f, cells - 1 : cells, lanes]
    spread(blocks, me, outs)


def pieces(group, width, rows):
    step = min(width, LANES)
    for d in range(group):
        for b in range(width // step):
            start = d * width + b * step
            yield d, b * rows, slice(start, start + step), slice(0, step)


class Lines:
    def __init__(self, ref, fields, cells, base):
        self.ref, self.fields, self.cells, self.base = ref, fields, cells, base

    def value(self, d, k, i):
        at = self.base(d) + k * self.fields * self.cells + i
        return self.ref[pl.ds(at, self.fields, stride=self.cells), :]

    def divided(self, d, i, value):
        if i == 1:
            return value
        at = self.base(d) + CELL_KINDS * self.fields * self.cells + (i if i == 0 else i - 1)
        return value * self.ref[pl.ds(at, self.fields, stride=self.cells + 1), :]


def less(value, factor, other):
    if other is None:
        return value
    return -(factor * other) if value is None else value - factor * other


SLOTS = 8


def sweep_kernel(group, fields, cells, me, half, table, *refs):
    jac, left = table_entries(table, fields, 0), table_entries(table, fields, 1)
    received, (lines, edge, message) = refs[:group], refs[group:]
    rows = block_rows(fields, cells)
    size = received[0].shape[0]
    count = size // rows
    for k in range(group):
        at = pl.multiple_of(lax.bitwise_xor(me[0], k) * size, SUBLANES)
        lines[pl.ds(at, size), :] = received[k][...]
    lower_half = jnp.full((fields, LANES), half[0], jnp.int32) == 0
    extra = CELL_KINDS * fields * cells
    for b in range(count):

        def across(row):
            return lines[pl.ds(b * rows + row, group, stride=size), :]

        firsts = [across(extra + f * (cells + 1) + cells - 1) for f in range(fields)]
        lasts = [across(extra + f * (cells + 1) + cells) for f in range(fields)]
        from_last = mix(jac, lasts)
        from_first = mix(jac, firsts)
        into_first = mix(left, [0.5 * x + dissipation * y for x, y in zip(from_last, lasts)])
        into_last = mix(left, [dissipation * y - 0.5 * x for x, y in zip(from_first, firsts)])
        at = 2 * b * fields * group
        for f in range(fields):
            edge[at + f * group : at + (f + 1) * group, :] = into_first[f]
            edge[at + (fields + f) * group : at + (fields + f + 1) * group, :] = into_last[f]

        def to_next(d):
            return edge[pl.ds(at + d, fields, stride=group), :]

        def to_previous(d):
            return edge[pl.ds(at + fields * group + d, fields, stride=group), :]

        view = Lines(lines, fields, cells, lambda d: (d * count + b) * rows)
        ones = jnp.ones((fields, LANES), jnp.float32)
        one, two = [None, ones, None], [None, None, None]
        forward = {}
        for d in range(group):
            for i in range(cells):
                value = view.value(d, 0, i)
                if i == 0 and d > 0:
                    value = value + to_next(d - 1)
                if i == cells - 1 and d < group - 1:
                    value = value + to_previous(d + 1)
                start = [value, None, ones if d == 0 and i == 0 else None]
                first, second = view.value(d, 1, i), view.value(d, 2, i)
                now = [less(less(start[c], second, two[c]), first, one[c]) for c in range(3)]
                forward[d, i] = now
                one, two = now, one
        ends = [one[0], two[0], to_next(group - 1)]
        one, two = [None] * 3, [None] * 3
        for d in reversed(range(group)):
            for i in reversed(range(cells)):
                start = [view.divided(d, i, value) for value in forward[d, i]]
                first, second = view.value(d, 3, i), view.value(d, 4, i)
                now = [less(less(start[c], second, two[c]), first, one[c]) for c in range(3)]
                one, two = now, one
        begins = [one[0], two[0], to_previous(0)]
        slots = [jnp.where(lower_half, x, y) for x, y in zip(ends, begins)]
        slots += [one[1], two[1], one[2], two[2], view.value(0, 2, 0)]
        for k, value in enumerate(slots):
            row = (b * SLOTS + k) * fields
            message[row : row + fields, :] = value


def solve_kernel(group, fields, cells, me, half, table, lines, edge, mine, other, *refs):
    outs, (squares, whole, blocks) = refs[:group], refs[group:]
    rows = block_rows(fields, cells)
    size = lines.shape[0] // group
    count = size // rows
    total = group * cells
    lower_half = jnp.full((fields, LANES), half[0], jnp.int32) == 0
    summed = None
    for b in range(count):
        view = Lines(lines, fields, cells, lambda d: (d * count + b) * rows)
        at = 2 * b * fields * group

        def to_next(d):
            return edge[pl.ds(at + d, fields, stride=group), :]

        def to_previous(d):
            return edge[pl.ds(at + fields * group + d, fields, stride=group), :]

        def slot(ref, k):
            row = (b * SLOTS + k) * fields
            return ref[row : row + fields, :]

        def of_lower(k):
            return jnp.where(lower_half, slot(mine, k), slot(other, k))

        def of_upper(k):
            return jnp.where(lower_half, slot(other, k), slot(mine, k))

        zeros = jnp.zeros((fields, LANES), jnp.float32)
        onto_last, onto_first = of_upper(2), of_lower(2)
        before, before_2 = of_lower(0) + onto_last, of_lower(1)
        added = onto_first - of_upper(7) * before_2
        after = of_upper(0) + of_upper(3) * before + of_upper(5) * added
        after_2 = of_upper(1) + of_upper(4) * before + of_upper(6) * added
        one, two = jnp.where(lower_half, zeros, before), jnp.where(lower_half, zeros, before_2)
        onto_first = jnp.where(lower_half, zeros, onto_first)
        onto_last = jnp.where(lower_half, onto_last, zeros)
        forward = {}
        for d in range(group):
            for i in range(cells):
                value = view.value(d, 0, i)
                if i == 0:
                    value = value + (to_next(d - 1) if d > 0 else onto_first)
                if i == cells - 1:
                    value = value + (to_previous(d + 1) if d < group - 1 else onto_last)
                value = less(less(value, view.value(d, 2, i), two), view.value(d, 1, i), one)
                forward[d, i] = value
                one, two = value, one
        one, two = jnp.where(lower_half, after, zeros), jnp.where(lower_half, after_2, zeros)
        for d in reversed(range(group)):
            for i in reversed(range(cells)):
                value = view.divided(d, i, forward[d, i])
                value = less(less(value, view.value(d, 4, i), two), view.value(d, 3, i), one)
                whole[pl.ds(b * fields * total + d * cells + i, fields, stride=total), :] = value
                one, two = value, one
        columns = [(b * fields + g) * total for g in range(fields)]
        increment = mix(table_entries(table, fields, 2), [whole[at : at + total, :] for at in columns])
        for f in range(fields):
            part = jnp.sum(increment[f] * increment[f], axis=0, keepdims=True)
            summed = part if summed is None else summed + part
            for d in range(group):
                row = (b * fields + f) * cells
                blocks[d, row : row + cells, :] = increment[f][d * cells : (d + 1) * cells, :]
    spread(blocks, me, outs)
    for n in range(squares.shape[0]):
        squares[n] = summed


def slab_kernel(peers, me, adj, grad, ctrl, *outs):
    fields, cells, length = adj.shape
    height = outs[0].shape[0]
    contribution = adj[0] * grad[0]
    for f in range(1, fields):
        contribution = contribution + adj[f] * grad[f]
    upper = contribution.astype(jnp.bfloat16).astype(jnp.float32)
    lower = contribution - upper
    high = lax.shift_right_logical(ctrl[...], 7)
    low = lax.bitwise_and(ctrl[...], LANES - 1)
    block = lax.broadcasted_iota(jnp.int32, (height, length), 0)
    lane = lax.broadcasted_iota(jnp.int32, (LANES, length), 0)
    sums = None
    for i in range(cells):
        hit = lane == low[i : i + 1, :]
        terms = jnp.concatenate(
            [
                jnp.where(hit, upper[i : i + 1, :], 0.0).astype(jnp.bfloat16),
                jnp.where(hit, lower[i : i + 1, :], 0.0).astype(jnp.bfloat16),
            ],
            axis=0,
        )
        rows = []
        for k in range(peers):
            offset = lax.bitwise_xor(me[0], k) * height
            rows.append(jnp.where(block == high[i : i + 1, :] - offset, 1.0, 0.0).astype(jnp.bfloat16))
        picked = jnp.concatenate(rows, axis=0)
        part = lax.dot_general(
            picked, terms, (((1,), (1,)), ((), ())), preferred_element_type=jnp.float32
        )
        sums = part if sums is None else sums + part
    sums = sums[:, :LANES] + sums[:, LANES:]
    for k in range(peers):
        outs[k][...] = sums[k * height : (k + 1) * height, :]


def finish_kernel(group, width, peers, cell_count, me, adj, squares, *refs):
    moved, slabs, (out, sens, blocks) = refs[:group], refs[group : group + peers], refs[group + peers :]
    fields, cells, _ = adj.shape
    for k in range(group):
        blocks[lax.bitwise_xor(me[0], k)] = moved[k][...]
    slab = slabs[0][...]
    for k in range(1, peers):
        slab = slab + slabs[k][...]
    sens[...] = slab
    total = jnp.sum(jnp.sum(squares[...], axis=0), axis=1, keepdims=True)
    factor = step_scale / jnp.sqrt(total / cell_count + epsilon)
    for d, base, lanes, to in pieces(group, width, fields * cells):
        for f in range(fields):
            at = base + f * cells
            out[f, :, lanes] = adj[f, :, lanes] + factor * blocks[d, at : at + cells, to]


def swap(array, axis, k):
    return lax.ppermute(array, axis, [(i, i ^ k) for i in range(lax.axis_size(axis))])


def exchange(arrays, axis):
    out = [arrays[0]]
    for k in range(1, len(arrays)):
        out.append(swap(arrays[k], axis, k))
    return out


def step(
    adjoint, source, shape_grad, lower_band, upper_band, jacobian, left_vectors, right_vectors, ctrl_local
):
    fields, cells, length = adjoint.shape
    parts, peers = lax.axis_size("stream"), lax.axis_size("cross")
    group = parts // 2
    width = length // group
    count = -(-width // LANES)
    rows = count * block_rows(fields, cells)
    back = count * fields * cells
    f32 = jnp.float32

    at = lax.axis_index("stream").astype(jnp.int32)
    me, half = lax.rem(at, group).reshape(1), lax.div(at, group).reshape(1)
    *packed, table = pl.pallas_call(
        functools.partial(pack_kernel, group, width),
        out_shape=[pltpu.VMEM((rows, LANES), f32)] * group
        + [pltpu.VMEM((table_rows(fields), LANES), f32)],
        in_specs=[SMEM] * 4 + [VMEM] * 4,
        out_specs=[VMEM] * (group + 1),
        scratch_shapes=[
            pltpu.VMEM((group, rows, LANES), f32),
            pltpu.VMEM((fields, round_up(cells + 2, SUBLANES), length), f32),
        ],
        name="pack",
    )(me, jacobian, left_vectors, right_vectors, adjoint, source, lower_band, upper_band)
    received = exchange(packed, "stream")

    height = NCTRL // (parts * peers * LANES)
    column = lax.axis_index("cross").astype(jnp.int32).reshape(1)
    slabs = pl.pallas_call(
        functools.partial(slab_kernel, peers),
        out_shape=[pltpu.VMEM((height, LANES), f32)] * peers,
        in_specs=[SMEM, VMEM, VMEM, VMEM],
        out_specs=[VMEM] * peers,
        cost_estimate=pl.CostEstimate(
            flops=4 * cells * length * NCTRL // parts, bytes_accessed=4 << 20, transcendentals=0
        ),
        name="slab",
    )(column, held(adjoint), shape_grad, ctrl_local)

    lines, edge, message = pl.pallas_call(
        functools.partial(sweep_kernel, group, fields, cells),
        out_shape=[
            pltpu.VMEM((group * rows, LANES), f32),
            pltpu.VMEM((2 * count * fields * group, LANES), f32),
            pltpu.VMEM((count * SLOTS * fields, LANES), f32),
        ],
        in_specs=[SMEM] * 2 + [VMEM] * (1 + group),
        out_specs=[VMEM] * 3,
        name="sweep",
    )(me, half, *(held(a) for a in (table, *received)))
    other = swap(message, "stream", group)
    slabs = exchange(slabs, "cross")

    *moved, squares = pl.pallas_call(
        functools.partial(solve_kernel, group, fields, cells),
        out_shape=[pltpu.VMEM((back, LANES), f32)] * group
        + [pltpu.VMEM((parts * peers, 1, LANES), f32)],
        in_specs=[SMEM] * 2 + [VMEM] * 5,
        out_specs=[VMEM] * (group + 1),
        scratch_shapes=[
            pltpu.VMEM((count * fields * group * cells, LANES), f32),
            pltpu.VMEM((group, back, LANES), f32),
        ],
        name="solve",
    )(me, half, *(held(a) for a in (table, lines, edge, message, other)))
    squares = lax.all_to_all(
        squares, ("stream", "cross"), split_axis=0, concat_axis=0, tiled=True,
        axis_index_groups=[list(range(parts * peers))[::-1]]
    )
    moved = exchange(moved, "stream")

    cell_count = fields * cells * length * parts * peers
    adjoint_next, sensitivity = pl.pallas_call(
        functools.partial(finish_kernel, group, width, peers, cell_count),
        out_shape=[
            jax.ShapeDtypeStruct(adjoint.shape, f32),
            jax.ShapeDtypeStruct((height, LANES), f32),
        ],
        in_specs=[SMEM] + [VMEM] * (2 + group + peers),
        out_specs=[VMEM, VMEM],
        scratch_shapes=[pltpu.VMEM((group, back, LANES), f32)],
        name="finish",
    )(me, *(held(a) for a in (adjoint, squares, *moved, *slabs)))
    return adjoint_next, sensitivity.reshape(height * LANES)


def solution(mesh):
    in_specs = (
        P(None, "stream", "cross"),
        P(None, "stream", "cross"),
        P(None, "stream", "cross"),
        P(None, None, "stream", "cross"),
        P(None, None, "stream", "cross"),
        P(),
        P(),
        P(),
        P("stream", "cross"),
    )
    out_specs = (P(None, "stream", "cross"), P(("stream", "cross")))
    return jax.shard_map(step, mesh=mesh, in_specs=in_specs, out_specs=out_specs, check_vma=False)
```
